256 devices in a mesh: seq: 64 (over y, z, core), head: 4 (over x).
Axes of the slice: x: 4, y: 4, z: 8, core: 2. Of those that a mesh axis runs over, the one named last changes fastest.
Arguments:
- queries: bfloat16 [16384, 32, 128], P('seq', 'head'), may hold values from -16 to 16
- keys: bfloat16 [16384, 32, 128], P('seq', 'head'), may hold values from -40 to 40
- values: bfloat16 [16384, 32, 128], P('seq', 'head'), may hold values from -6 to 6
- cluster_ids: int32 [16384, 32], P('seq', 'head'), may hold values from 0 to 511, as said below
- out_weight: bfloat16 [4096, 4096], P('seq', 'head'), may hold values from -0.09375 to 0.09375
Outputs:
- mixed: bfloat16 [16384, 4096], P('seq', 'head')
The draws below stay inside these ranges and needn't reach their ends.
Inputs may be any that keep to these rules, and one draw needn't show every extreme that they name: `cluster_ids`: in each head h, the ids j with j % 16 equal to one residue, drawn from the seed for that head, are never used.
All inputs are finite; a program needn't handle non-finite values.
Results may differ from the reference program's by a relative error of at most 0.008.
The reference program's roundings to bfloat16 on the way (of `centroid`, `attended` and `features`) count: a program that leaves them out, or rounds other values in their place, can miss the bound.
Values may be sent and summed in bfloat16 or wider, within the bound.
A program may use at most 320 MiB of HBM per device.

```python
import math
import jax
import jax.numpy as jnp
from jax import lax

HEADS = 32
E = 128
C = 512
D = 4096
TOKENS = 16384


def make_ids(key):
    base = jax.random.fold_in(key, 101)
    raw = jax.random.randint(jax.random.fold_in(base, 1), (TOKENS, HEADS), 0, C)
    skipped = jax.random.randint(jax.random.fold_in(base, 2), (HEADS,), 0, 16)
    hit = raw % 16 == skipped[None, :]
    return jnp.where(hit, jnp.bitwise_xor(raw, 1), raw).astype(jnp.int32)


def make_centers(key):
    draws = jax.random.normal(jax.random.fold_in(key, 111), (HEADS, C, E), jnp.float32)
    return 3.0 * jnp.clip(draws, -4.0, 4.0)


def draw_cluster_ids(key, part):
    return make_ids(key)


def draw_queries(key, part):
    labels = make_ids(key)
    centers = make_centers(key)
    noise = jnp.clip(jax.random.normal(jax.random.fold_in(key, 201), (TOKENS, HEADS, E), jnp.float32), -4.0, 4.0)
    picked = centers[jnp.arange(HEADS)[None, :], labels]
    return (noise + picked).astype(jnp.bfloat16)


def draw_keys(key, part):
    result = jnp.clip(jax.random.normal(jax.random.fold_in(key, 301), (TOKENS, HEADS, E), jnp.float32), -4.0, 4.0)
    return result.astype(jnp.bfloat16)


def level_of(key, shape, cuts, low, largest):
    factor_of, own = 1.0, jax.random.fold_in(key, 6)
    for axis_at, parts in cuts:
        heights = jnp.exp(jax.random.uniform(jax.random.fold_in(own, axis_at), (parts,), jnp.float32, low / len(cuts), largest / len(cuts)))
        factor_of = factor_of * jnp.repeat(heights, shape[axis_at] // parts).reshape([-1 if axis == axis_at else 1 for axis in range(len(shape))])
    return factor_of


def bell_draw(key, dims, scale, limit, shards=(), kind=jnp.bfloat16):
    entries = jax.random.normal(key, dims, jnp.float32) * scale
    if len(shards) > 0:
        entries = level_of(key, dims, shards, -0.22, 0.18) * entries
    return jnp.clip(entries, min=-limit, max=limit).astype(kind)


def setup_inputs(seed: int = 0) -> dict:
    arg_keys = jax.random.split(jax.random.key(seed), 6)
    return {
        "queries": draw_queries(jax.random.fold_in(arg_keys[5], 71), 0),
        "keys": draw_keys(jax.random.fold_in(arg_keys[5], 71), 0),
        "values": bell_draw(arg_keys[2], (TOKENS, HEADS, E), 1.0, 6.0, ((0, 64), (1, 4))),
        "cluster_ids": draw_cluster_ids(jax.random.fold_in(arg_keys[5], 71), 0),
        "out_weight": bell_draw(arg_keys[4], (D, D), D ** -0.5, 0.09375, ((0, 64), (1, 4))),
    }


def one_head(operands):
    q_head, k_head, v_head, id_head = operands
    ones = jnp.ones((q_head.shape[0],), jnp.float32)
    counts = jax.ops.segment_sum(ones, id_head, num_segments=C)
    totals = jax.ops.segment_sum(q_head.astype(jnp.float32), id_head, num_segments=C)
    centroid = (totals / jnp.maximum(counts, 1.0)[:, None]).astype(jnp.bfloat16)
    scores = jnp.dot(centroid, k_head.T, preferred_element_type=jnp.float32) * (1.0 / math.sqrt(E))
    top = lax.optimization_barrier(jnp.max(scores, axis=1))
    weights = jnp.exp(scores - top[:, None])
    total = lax.optimization_barrier(jnp.sum(weights, axis=1))
    summed = jnp.dot(weights.astype(jnp.bfloat16), v_head, preferred_element_type=jnp.float32)
    attended = (summed / total[:, None]).astype(jnp.bfloat16)
    return attended[id_head]

def reference(queries, keys, values, cluster_ids, out_weight):
    heads_out = lax.map(one_head, (jnp.transpose(queries, (1, 0, 2)), jnp.transpose(keys, (1, 0, 2)), jnp.transpose(values, (1, 0, 2)), cluster_ids.T))
    features = jnp.transpose(heads_out, (1, 0, 2)).reshape(queries.shape[0], HEADS * E)
    return jnp.dot(features, out_weight, preferred_element_type=jnp.float32).astype(jnp.bfloat16)
```

```python
import math

import jax
import jax.numpy as jnp
from jax import lax
from jax.experimental import pallas as pl
from jax.experimental.pallas import tpu as pltpu
from jax.sharding import PartitionSpec as P

C = 512
E = 128
NY, NZ, NX = 4, 8, 4
TOK = 256
BLK = C // NZ
ROWS = BLK + 8
EXP2_SCALE = math.log2(math.e) / math.sqrt(E)
F32, BF16 = jnp.float32, jnp.bfloat16


def chain_kernel(
    q_ref, k_ref, v_ref, ids_ref, idx_ref, out_ref,
    qbuf, kbuf, vbuf, idbuf, idxbuf, acc, msg, recv_t, recv_o, cent, sbuf, mx, ls,
    att, idcol, fsend, frecv,
    ssem, rq, rk, rv, rid, ridx, rt, rc, ro, rz, ra, rb, rf, lsem,
):
    s_id, x = lax.axis_index("seq"), lax.axis_index("head")
    c = lax.rem(s_id, 2)
    z = lax.rem(lax.div(s_id, 2), NZ)
    y = lax.div(s_id, 2 * NZ)
    yc = y * 2 + c
    g0 = x * NY + y

    def seq_of(yy, zz, cc):
        return (yy * NZ + zz) * 2 + cc

    sends = []

    def put(src, dst, rsem, seq, head):
        cp = pltpu.make_async_remote_copy(
            src_ref=src, dst_ref=dst, send_sem=ssem.at[len(sends)], recv_sem=rsem,
            device_id=(seq, head), device_id_type=pl.DeviceIdType.MESH,
        )
        cp.start()
        sends.append(cp)
        return cp

    def arrived(ref, rsem):
        pltpu.make_async_copy(ref, ref, rsem).wait()

    def yc_peer(d):
        t = lax.rem(yc + d, 8)
        return lax.div(t, 2), lax.rem(t, 2)

    barrier = pltpu.get_barrier_semaphore()

    def greet(seq, head):
        pl.semaphore_signal(barrier, inc=1, device_id=(seq, head), device_id_type=pl.DeviceIdType.MESH)

    for d in range(1, 8):
        ty, tc = yc_peer(d)
        greet(seq_of(ty, z, tc), x)
        greet(seq_of(y, lax.rem(z + d, NZ), c), x)
    for e in range(1, NX):
        greet(s_id, lax.rem(x + e, NX))
        greet(seq_of(y, z, 1 - c), lax.rem(x + e, NX))

    local = []
    own_h = c * NY + y
    for n, (src, dst) in enumerate(
        ((ids_ref.at[own_h], idbuf.at[yc]), (q_ref.at[own_h], qbuf.at[yc]),
         (k_ref.at[own_h], kbuf.at[yc]), (v_ref.at[own_h], vbuf.at[yc]),
         (idx_ref.at[c], idxbuf.at[c]))
    ):
        cp = pltpu.make_async_copy(src, dst, lsem.at[n])
        cp.start()
        local.append(cp)

    pl.semaphore_wait(barrier, 20)

    for src, buf, sem in ((ids_ref, idbuf, rid), (q_ref, qbuf, rq)):
        for d in range(1, 8):
            ty, tc = yc_peer(d)
            put(src.at[tc * NY + ty], buf.at[yc], sem.at[d - 1], seq_of(ty, z, tc), x)
    put(idx_ref.at[1 - c], idxbuf.at[c], ridx.at[1], seq_of(y, z, 1 - c), x)
    for e in range(1, NX):
        for f in range(2):
            tc = lax.rem(c + f, 2)
            put(idx_ref.at[tc], idxbuf.at[(NX - e) * 2 + c], ridx.at[(NX - e) * 2 + f],
                seq_of(y, z, tc), lax.rem(x + e, NX))
    for src, buf, sem in ((k_ref, kbuf, rk), (v_ref, vbuf, rv)):
        for d in range(1, 8):
            ty, tc = yc_peer(d)
            put(src.at[tc * NY + ty], buf.at[yc], sem.at[d - 1], seq_of(ty, z, tc), x)

    def take8(buf, sem):
        for d in range(1, 8):
            arrived(buf.at[lax.rem(yc + 8 - d, 8)], sem.at[d - 1])

    eye = lax.broadcasted_iota(jnp.int32, (BLK, E), 0) == lax.broadcasted_iota(jnp.int32, (BLK, E), 1)

    def to_row(col):
        return jnp.sum(jnp.where(eye, col, 0.0), axis=0, keepdims=True)

    def to_col(row):
        return jnp.sum(jnp.where(eye, row, 0.0), axis=1, keepdims=True)

    local[0].wait()
    local[1].wait()
    take8(idbuf, rid)
    take8(qbuf, rq)
    acc[...] = jnp.zeros_like(acc)

    @pl.loop(0, 8)
    def _(i):
        label = lax.broadcasted_iota(jnp.int32, (C, TOK), 0)
        onehot = (label == idbuf[i]).astype(F32).astype(BF16)
        rhs = jnp.concatenate([qbuf[i], jnp.ones((TOK, E), BF16)], axis=1)
        acc[...] += jnp.dot(onehot, rhs, preferred_element_type=F32)

    @pl.loop(0, NZ)
    def _(b):
        rows = pl.ds(pl.multiple_of(b * BLK, BLK), BLK)
        msg[b, pl.ds(0, BLK), :] = acc[rows, pl.ds(0, E)]
        row = to_row(acc[rows, pl.ds(E, E)])
        msg[b, pl.ds(BLK, 8), :] = jnp.broadcast_to(row, (8, E))

    def reduce_z(recv, sem, src):
        for d in range(1, NZ):
            tz = lax.rem(z + d, NZ)
            put(src.at[tz], recv.at[d - 1], sem.at[d - 1], seq_of(y, tz, c), x)

    reduce_z(recv_t, rt, msg.at[pl.ds(0, NZ)])

    local[4].wait()
    for j in range(1, 8):
        e, f = j // 2, j % 2
        arrived(idxbuf.at[e * 2 + lax.rem(c + f, 2)], ridx.at[j])
    for half in range(2):
        rows = jnp.concatenate([idxbuf[e * 2 + half] for e in range(NX)], axis=0).astype(F32)
        rows = jnp.concatenate([rows, jnp.zeros((E - 8 * NX, TOK), F32)], axis=0)
        idcol[pl.ds(half * TOK, TOK), :] = rows.T

    total = msg[z]
    for d in range(1, NZ):
        arrived(recv_t.at[d - 1], rt.at[d - 1])
        total = total + recv_t[d - 1]
    count = to_col(total[BLK:BLK + 1, :])
    cent[z] = (total[:BLK, :] / jnp.maximum(count, 1.0)).astype(BF16)

    def gather_z(buf, sem):
        for d in range(1, NZ):
            tz = lax.rem(z + d, NZ)
            put(buf.at[z], buf.at[z], sem.at[d - 1], seq_of(y, tz, c), x)

    gather_z(cent, rc)
    local[2].wait()
    take8(kbuf, rk)
    for d in range(1, NZ):
        arrived(cent.at[lax.rem(z + NZ - d, NZ)], rc.at[d - 1])

    centroid = cent[...].reshape(C, E)
    mx[...] = jnp.full_like(mx, -jnp.inf)

    @pl.loop(0, 8)
    def _(i):
        s = lax.dot_general(centroid, kbuf[i], (((1,), (1,)), ((), ())), preferred_element_type=F32)
        sbuf[i] = s
        mx[...] = jnp.maximum(mx[...], jnp.maximum(s[:, :E], s[:, E:]))

    top = jnp.broadcast_to(jnp.max(mx[...], axis=1, keepdims=True), (C, E))
    mx[...] = top
    ls[...] = jnp.zeros_like(ls)
    acc[:, pl.ds(0, E)] = jnp.zeros((C, E), F32)
    local[3].wait()
    take8(vbuf, rv)

    @pl.loop(0, 8)
    def _(i):
        m = mx[...]
        p = jnp.exp2((sbuf[i] - jnp.concatenate([m, m], axis=1)) * EXP2_SCALE)
        ls[...] += p[:, :E] + p[:, E:]
        acc[:, pl.ds(0, E)] += jnp.dot(p.astype(BF16), vbuf[i], preferred_element_type=F32)

    ls[...] = jnp.broadcast_to(jnp.sum(ls[...], axis=1, keepdims=True), (C, E))

    @pl.loop(0, NZ)
    def _(b):
        rows = pl.ds(pl.multiple_of(b * BLK, BLK), BLK)
        msg[NZ + b, pl.ds(0, BLK), :] = acc[rows, pl.ds(0, E)]
        first = lax.broadcasted_iota(jnp.int32, (8, E), 0) == 0
        msg[NZ + b, pl.ds(BLK, 8), :] = jnp.where(first, to_row(mx[rows, :]), to_row(ls[rows, :]))

    reduce_z(recv_o, ro, msg.at[pl.ds(NZ, NZ)])
    parts = [msg[NZ + z]]
    for d in range(1, NZ):
        arrived(recv_o.at[d - 1], ro.at[d - 1])
        parts.append(recv_o[d - 1])
    tops = [to_col(part[BLK:BLK + 1, :]) for part in parts]
    largest = tops[0]
    for t in tops[1:]:
        largest = jnp.maximum(largest, t)
    num, den = 0.0, 0.0
    for part, t in zip(parts, tops):
        factor = jnp.exp2((t - largest) * EXP2_SCALE)
        num = num + part[:BLK, :] * factor
        den = den + to_col(part[BLK + 1:BLK + 2, :]) * factor
    att[g0, z] = (num / den).astype(BF16)

    for d in range(1, NZ):
        tz = lax.rem(z + d, NZ)
        put(att.at[g0, z], att.at[g0, z], rz.at[d - 1], seq_of(y, tz, c), x)
    for d in range(1, NZ):
        arrived(att.at[g0, lax.rem(z + NZ - d, NZ)], rz.at[d - 1])

    low, high = pl.ds(0, NZ // 2), pl.ds(NZ // 2, NZ // 2)

    def g_of(dx, dy):
        return lax.rem(x + dx, NX) * NY + lax.rem(y + dy, NY)

    def to_y(g, part, sem, dx):
        for e in range(1, NY):
            put(att.at[g, part], att.at[g, part], sem.at[dx * NY + NY - e],
                seq_of(lax.rem(y + e, NY), z, c), x)

    def to_x(g, part, sem, dy):
        for e in range(1, NX):
            put(att.at[g, part], att.at[g, part], sem.at[(NX - e) * NY + dy],
                s_id, lax.rem(x + e, NX))

    to_y(g0, low, ra, 0)
    to_x(g0, high, rb, 0)
    to_x(g0, low, ra, 0)
    to_y(g0, high, rb, 0)
    for e in range(1, NY):
        arrived(att.at[g_of(0, e), low], ra.at[e])
        to_x(g_of(0, e), low, ra, e)
        arrived(att.at[g_of(e, 0), high], rb.at[e * NY])
        to_y(g_of(e, 0), high, rb, e)

    lanes = lax.broadcasted_iota(jnp.int32, (2 * TOK, C), 1).astype(F32)
    own = pl.ds(pl.multiple_of(c * TOK, TOK), TOK)
    fcopies = []
    for dx in range(NX):
        xs = lax.rem(x + dx, NX)
        for dy in range(NY):
            g = g_of(dx, dy)
            if dx > 0:
                arrived(att.at[g, low], ra.at[dx * NY + dy])
            if dy > 0:
                arrived(att.at[g, high], rb.at[dx * NY + dy])
            col = idcol[:, pl.ds(dx * 8 + dy, 1)]
            onehot = (lanes == col).astype(F32).astype(BF16)
            feat = jnp.dot(onehot, att[g].reshape(C, E), preferred_element_type=F32).astype(BF16)
            acc_rows = pl.ds(pl.multiple_of((xs * 8 + c * NY + lax.rem(y + dy, NY)) * E, E), E)
            send_cols = pl.ds(pl.multiple_of(g * E, E), E)
            mine = jnp.where(c == 0, feat[:TOK], feat[TOK:])
            theirs = jnp.where(c == 0, feat[TOK:], feat[:TOK])
            out_ref[:, acc_rows] = mine
            fsend[:, send_cols] = theirs
        cols = pl.ds(pl.multiple_of(xs * NY * E, NY * E), NY * E)
        put(fsend.at[:, cols], frecv.at[:, cols], rf.at[dx], seq_of(y, z, 1 - c), x)
    for dx in range(NX):
        xs = lax.rem(x + dx, NX)
        cols = pl.ds(pl.multiple_of(xs * NY * E, NY * E), NY * E)
        arrived(frecv.at[:, cols], rf.at[dx])
        there = pl.ds(pl.multiple_of(xs * 8 * E + (1 - c) * NY * E, NY * E), NY * E)
        out_ref[:, there] = frecv[:, cols]
    for cp in sends:
        cp.wait_send()


def chain(queries, keys, values, ids, idx):
    vmem = pl.BlockSpec(memory_space=pltpu.VMEM)
    anyw = pl.BlockSpec(memory_space=pl.ANY)
    dma = pltpu.SemaphoreType.DMA
    return pl.pallas_call(
        chain_kernel,
        out_shape=jax.ShapeDtypeStruct((TOK, 32 * E), BF16),
        in_specs=[anyw, anyw, anyw, vmem, vmem],
        out_specs=vmem,
        scratch_shapes=[
            pltpu.VMEM((8, TOK, E), BF16), pltpu.VMEM((8, TOK, E), BF16), pltpu.VMEM((8, TOK, E), BF16),
            pltpu.VMEM((8, 1, TOK), jnp.int32), pltpu.VMEM((8, 8, TOK), jnp.int32),
            pltpu.VMEM((C, 2 * E), F32), pltpu.VMEM((2 * NZ, ROWS, E), F32),
            pltpu.VMEM((NZ - 1, ROWS, E), F32), pltpu.VMEM((NZ - 1, ROWS, E), F32),
            pltpu.VMEM((NZ, BLK, E), BF16), pltpu.VMEM((8, C, TOK), F32),
            pltpu.VMEM((C, E), F32), pltpu.VMEM((C, E), F32),
            pltpu.VMEM((16, NZ, BLK, E), BF16), pltpu.VMEM((2 * TOK, E), F32),
            pltpu.VMEM((TOK, 16 * E), BF16), pltpu.VMEM((TOK, 16 * E), BF16),
            dma((112,)), dma((7,)), dma((7,)), dma((7,)), dma((7,)), dma((8,)), dma((7,)), dma((7,)),
            dma((7,)), dma((7,)), dma((16,)), dma((16,)), dma((4,)), dma((5,)),
        ],
        compiler_params=pltpu.CompilerParams(
            collective_id=0, has_side_effects=True, vmem_limit_bytes=48 * 1024 * 1024
        ),
        cost_estimate=pl.CostEstimate(flops=4_000_000_000, bytes_accessed=200_000_000, transcendentals=1 << 20),
    )(queries, keys, values, ids, idx)


def on_device(queries, keys, values, cluster_ids, out_weight):
    y = lax.div(lax.axis_index("seq"), 2 * NZ)
    ids = cluster_ids.T
    pair = ids.reshape(2, NY, TOK)
    pair = lax.dynamic_slice_in_dim(jnp.concatenate([pair, pair], axis=1), y, NY, axis=1)
    idx = jnp.concatenate([pair, jnp.zeros_like(pair)], axis=1)
    weight = lax.all_gather(out_weight, "seq", axis=0, tiled=True)
    q, k, v = (jnp.transpose(a, (1, 0, 2)) for a in (queries, keys, values))
    features = chain(q, k, v, ids[:, None, :], idx)
    mixed = jnp.dot(features, weight, preferred_element_type=F32)
    return mixed.astype(BF16)


def solution(mesh):
    placed = (
        P("seq", "head", None),
        P("seq", "head", None),
        P("seq", "head", None),
        P("seq", "head"),
        P("seq", "head"),
    )
    return jax.shard_map(
        on_device, mesh=mesh, in_specs=placed, out_specs=P("seq", "head"), check_vma=False
    )
```

```python
import math

import jax
import jax.numpy as jnp
from jax import lax
from jax.experimental import pallas as pl
from jax.experimental.pallas import tpu as pltpu
from jax.sharding import PartitionSpec as P

C = 512
E = 128
NY, NZ, NX = 4, 8, 4
TOK = 256
BLK = C // NZ
ROWS = BLK + 8
HALF = E // 2
EXP2_SCALE = math.log2(math.e) / math.sqrt(E)
F32, BF16 = jnp.float32, jnp.bfloat16


def chain_kernel(
    q_ref, k_ref, v_ref, ids_ref, idx_ref, w_ref, out_ref,
    qbuf, kbuf, vbuf, idbuf, idxbuf, acc, msg, recv_t, recv_o, cent, sbuf, mx, ls,
    att, idcol, wbuf, feat, psum, other,
    ssem, rq, rk, rv, rid, ridx, rt, rc, ro, rz, ra, rb, rf, lsem, swc, rwo, rw1, rwr, rwl, rwy,
):
    s_id, x = lax.axis_index("seq"), lax.axis_index("head")
    c = lax.rem(s_id, 2)
    z = lax.rem(lax.div(s_id, 2), NZ)
    y = lax.div(s_id, 2 * NZ)
    yc = y * 2 + c
    g0 = x * NY + y

    def seq_of(yy, zz, cc):
        return (yy * NZ + zz) * 2 + cc

    sends = []

    def put(src, dst, rsem, seq, head):
        cp = pltpu.make_async_remote_copy(
            src_ref=src, dst_ref=dst, send_sem=ssem.at[len(sends)], recv_sem=rsem,
            device_id=(seq, head), device_id_type=pl.DeviceIdType.MESH,
        )
        cp.start()
        sends.append(cp)
        return cp

    maybe = []

    def put_if(cond, src, dst, rsem, seq, head):
        cp = pltpu.make_async_remote_copy(
            src_ref=src, dst_ref=dst, send_sem=swc.at[len(maybe)], recv_sem=rsem,
            device_id=(seq, head), device_id_type=pl.DeviceIdType.MESH,
        )
        pl.when(cond)(cp.start)
        maybe.append((cond, cp))

    def arrived(ref, rsem):
        pltpu.make_async_copy(ref, ref, rsem).wait()

    def yc_peer(d):
        t = lax.rem(yc + d, 8)
        return lax.div(t, 2), lax.rem(t, 2)

    barrier = pltpu.get_barrier_semaphore()

    def greet(seq, head):
        pl.semaphore_signal(barrier, inc=1, device_id=(seq, head), device_id_type=pl.DeviceIdType.MESH)

    for d in range(1, 8):
        ty, tc = yc_peer(d)
        greet(seq_of(ty, z, tc), x)
        greet(seq_of(y, lax.rem(z + d, NZ), c), x)
    for step in (1, NZ - 1):
        greet(seq_of(y, lax.rem(z + step, NZ), 1 - c), x)
    for e in range(1, NX):
        greet(s_id, lax.rem(x + e, NX))
        greet(seq_of(y, z, 1 - c), lax.rem(x + e, NX))

    local = []
    own_h = c * NY + y
    for n, (src, dst) in enumerate(
        ((ids_ref.at[own_h], idbuf.at[yc]), (q_ref.at[own_h], qbuf.at[yc]),
         (k_ref.at[own_h], kbuf.at[yc]), (v_ref.at[own_h], vbuf.at[yc]),
         (idx_ref.at[c], idxbuf.at[c]))
    ):
        cp = pltpu.make_async_copy(src, dst, lsem.at[n])
        cp.start()
        local.append(cp)

    pl.semaphore_wait(barrier, 22)

    for src, buf, sem in ((ids_ref, idbuf, rid), (q_ref, qbuf, rq)):
        for d in range(1, 8):
            ty, tc = yc_peer(d)
            put(src.at[tc * NY + ty], buf.at[yc], sem.at[d - 1], seq_of(ty, z, tc), x)
    put(idx_ref.at[1 - c], idxbuf.at[c], ridx.at[1], seq_of(y, z, 1 - c), x)
    for e in range(1, NX):
        for f in range(2):
            tc = lax.rem(c + f, 2)
            put(idx_ref.at[tc], idxbuf.at[(NX - e) * 2 + c], ridx.at[(NX - e) * 2 + f],
                seq_of(y, z, tc), lax.rem(x + e, NX))
    for src, buf, sem in ((k_ref, kbuf, rk), (v_ref, vbuf, rv)):
        for d in range(1, 8):
            ty, tc = yc_peer(d)
            put(src.at[tc * NY + ty], buf.at[yc], sem.at[d - 1], seq_of(ty, z, tc), x)

    home = lax.div(z, NZ // 2)
    half_rows = pl.ds(pl.multiple_of(c * HALF, HALF), HALF)
    other_rows = pl.ds(pl.multiple_of((1 - c) * HALF, HALF), HALF)

    def w_slot(o):
        return y * NY + lax.rem(o, NY)

    def w_held(o):
        return lax.div(o, NZ // 2) == c

    w_own = wbuf.at[w_slot(z), half_rows]
    w_copy = pltpu.make_async_copy(w_ref, w_own, lsem.at[5])
    pl.when(home == c)(w_copy.start)
    put_if(home != c, w_ref, w_own, rwo, seq_of(y, z, 1 - c), x)
    for step, sem in ((1, 0), (NZ - 1, 2)):
        put(w_ref, w_own, rw1.at[sem + c], seq_of(y, lax.rem(z + step, NZ), home), x)

    def w_turn(k, far, sems, base):
        o = lax.rem(z + far * k, NZ)
        slot = w_slot(o)
        if k == 1:
            @pl.when(w_held(o))
            def _():
                for cc in range(2):
                    arrived(wbuf.at[slot, pl.ds(cc * HALF, HALF)], rw1.at[base + cc])
        else:
            @pl.when(w_held(o))
            def _():
                arrived(wbuf.at[slot], sems.at[k - 2])
        return o, slot

    def w_step(k):
        o, slot = w_turn(k, NZ - 1, rwr, 0)
        put_if(w_held(o), wbuf.at[slot], wbuf.at[slot], rwr.at[k - 1], seq_of(y, lax.rem(z + 1, NZ), c), x)
        if k < 3:
            o, slot = w_turn(k, 1, rwl, 2)
            put_if(w_held(o), wbuf.at[slot], wbuf.at[slot], rwl.at[k - 1],
                   seq_of(y, lax.rem(z + NZ - 1, NZ), c), x)

    def w_spread():
        w_turn(4, NZ - 1, rwr, 0)
        w_turn(3, 1, rwl, 2)

        @pl.when(home == c)
        def _():
            w_copy.wait()
            arrived(wbuf.at[w_slot(z), other_rows], rwo)

        up, down = seq_of(lax.rem(y + 1, NY), z, c), seq_of(lax.rem(y + NY - 1, NY), z, c)
        for n, (lo, to) in enumerate(((0, up), (2, down), (2, up), (0, down))):
            rows = wbuf.at[pl.ds(y * NY + lo, 2)]
            put(rows, rows, rwy.at[n], to, x)

    def w_relay():
        below, above = lax.rem(y + NY - 1, NY), lax.rem(y + 1, NY)
        first = wbuf.at[pl.ds(below * NY, 2)]
        arrived(first, rwy.at[0])
        put(first, first, rwy.at[4], seq_of(above, z, c), x)
        second = wbuf.at[pl.ds(above * NY + 2, 2)]
        arrived(second, rwy.at[1])
        put(second, second, rwy.at[5], seq_of(below, z, c), x)

    def w_finish():
        below, above, across = lax.rem(y + NY - 1, NY), lax.rem(y + 1, NY), lax.rem(y + 2, NY)
        arrived(wbuf.at[pl.ds(below * NY + 2, 2)], rwy.at[2])
        arrived(wbuf.at[pl.ds(above * NY, 2)], rwy.at[3])
        arrived(wbuf.at[pl.ds(across * NY, 2)], rwy.at[4])
        arrived(wbuf.at[pl.ds(across * NY + 2, 2)], rwy.at[5])

    def take8(buf, sem):
        for d in range(1, 8):
            arrived(buf.at[lax.rem(yc + 8 - d, 8)], sem.at[d - 1])

    eye = lax.broadcasted_iota(jnp.int32, (BLK, E), 0) == lax.broadcasted_iota(jnp.int32, (BLK, E), 1)

    def to_row(col):
        return jnp.sum(jnp.where(eye, col, 0.0), axis=0, keepdims=True)

    def to_col(row):
        return jnp.sum(jnp.where(eye, row, 0.0), axis=1, keepdims=True)

    local[0].wait()
    local[1].wait()
    take8(idbuf, rid)
    take8(qbuf, rq)
    w_step(1)
    acc[...] = jnp.zeros_like(acc)

    @pl.loop(0, 8)
    def _(i):
        label = lax.broadcasted_iota(jnp.int32, (C, TOK), 0)
        onehot = (label == idbuf[i]).astype(F32).astype(BF16)
        rhs = jnp.concatenate([qbuf[i], jnp.ones((TOK, E), BF16)], axis=1)
        acc[...] += jnp.dot(onehot, rhs, preferred_element_type=F32)

    @pl.loop(0, NZ)
    def _(b):
        rows = pl.ds(pl.multiple_of(b * BLK, BLK), BLK)
        msg[b, pl.ds(0, BLK), :] = acc[rows, pl.ds(0, E)]
        row = to_row(acc[rows, pl.ds(E, E)])
        msg[b, pl.ds(BLK, 8), :] = jnp.broadcast_to(row, (8, E))

    def reduce_z(recv, sem, src):
        for d in range(1, NZ):
            tz = lax.rem(z + d, NZ)
            put(src.at[tz], recv.at[d - 1], sem.at[d - 1], seq_of(y, tz, c), x)

    reduce_z(recv_t, rt, msg.at[pl.ds(0, NZ)])
    w_step(2)

    local[4].wait()
    for j in range(1, 8):
        e, f = j // 2, j % 2
        arrived(idxbuf.at[e * 2 + lax.rem(c + f, 2)], ridx.at[j])
    for half in range(2):
        rows = jnp.concatenate([idxbuf[e * 2 + half] for e in range(NX)], axis=0).astype(F32)
        rows = jnp.concatenate([rows, jnp.zeros((E - 8 * NX, TOK), F32)], axis=0)
        idcol[pl.ds(half * TOK, TOK), :] = rows.T

    total = msg[z]
    for d in range(1, NZ):
        arrived(recv_t.at[d - 1], rt.at[d - 1])
        total = total + recv_t[d - 1]
    count = to_col(total[BLK:BLK + 1, :])
    cent[z] = (total[:BLK, :] / jnp.maximum(count, 1.0)).astype(BF16)

    def gather_z(buf, sem):
        for d in range(1, NZ):
            tz = lax.rem(z + d, NZ)
            put(buf.at[z], buf.at[z], sem.at[d - 1], seq_of(y, tz, c), x)

    gather_z(cent, rc)
    w_step(3)
    local[2].wait()
    take8(kbuf, rk)
    for d in range(1, NZ):
        arrived(cent.at[lax.rem(z + NZ - d, NZ)], rc.at[d - 1])

    w_spread()
    centroid = cent[...].reshape(C, E)
    mx[...] = jnp.full_like(mx, -jnp.inf)

    @pl.loop(0, 8)
    def _(i):
        s = lax.dot_general(centroid, kbuf[i], (((1,), (1,)), ((), ())), preferred_element_type=F32)
        sbuf[i] = s
        mx[...] = jnp.maximum(mx[...], jnp.maximum(s[:, :E], s[:, E:]))

    top = jnp.broadcast_to(jnp.max(mx[...], axis=1, keepdims=True), (C, E))
    mx[...] = top
    ls[...] = jnp.zeros_like(ls)
    acc[:, pl.ds(0, E)] = jnp.zeros((C, E), F32)
    local[3].wait()
    take8(vbuf, rv)

    @pl.loop(0, 8)
    def _(i):
        m = mx[...]
        p = jnp.exp2((sbuf[i] - jnp.concatenate([m, m], axis=1)) * EXP2_SCALE)
        ls[...] += p[:, :E] + p[:, E:]
        acc[:, pl.ds(0, E)] += jnp.dot(p.astype(BF16), vbuf[i], preferred_element_type=F32)

    ls[...] = jnp.broadcast_to(jnp.sum(ls[...], axis=1, keepdims=True), (C, E))

    @pl.loop(0, NZ)
    def _(b):
        rows = pl.ds(pl.multiple_of(b * BLK, BLK), BLK)
        msg[NZ + b, pl.ds(0, BLK), :] = acc[rows, pl.ds(0, E)]
        first = lax.broadcasted_iota(jnp.int32, (8, E), 0) == 0
        msg[NZ + b, pl.ds(BLK, 8), :] = jnp.where(first, to_row(mx[rows, :]), to_row(ls[rows, :]))

    reduce_z(recv_o, ro, msg.at[pl.ds(NZ, NZ)])
    parts = [msg[NZ + z]]
    for d in range(1, NZ):
        arrived(recv_o.at[d - 1], ro.at[d - 1])
        parts.append(recv_o[d - 1])
    tops = [to_col(part[BLK:BLK + 1, :]) for part in parts]
    largest = tops[0]
    for t in tops[1:]:
        largest = jnp.maximum(largest, t)
    num, den = 0.0, 0.0
    for part, t in zip(parts, tops):
        factor = jnp.exp2((t - largest) * EXP2_SCALE)
        num = num + part[:BLK, :] * factor
        den = den + to_col(part[BLK + 1:BLK + 2, :]) * factor
    att[g0, z] = (num / den).astype(BF16)

    for d in range(1, NZ):
        tz = lax.rem(z + d, NZ)
        put(att.at[g0, z], att.at[g0, z], rz.at[d - 1], seq_of(y, tz, c), x)
    w_relay()
    for d in range(1, NZ):
        arrived(att.at[g0, lax.rem(z + NZ - d, NZ)], rz.at[d - 1])

    low, high = pl.ds(0, NZ // 2), pl.ds(NZ // 2, NZ // 2)

    def g_of(dx, dy):
        return lax.rem(x + dx, NX) * NY + lax.rem(y + dy, NY)

    def to_y(g, part, sem, dx):
        for e in range(1, NY):
            put(att.at[g, part], att.at[g, part], sem.at[dx * NY + NY - e],
                seq_of(lax.rem(y + e, NY), z, c), x)

    def to_x(g, part, sem, dy):
        for e in range(1, NX):
            put(att.at[g, part], att.at[g, part], sem.at[(NX - e) * NY + dy],
                s_id, lax.rem(x + e, NX))

    to_y(g0, low, ra, 0)
    to_x(g0, high, rb, 0)
    to_x(g0, low, ra, 0)
    to_y(g0, high, rb, 0)
    for e in range(1, NY):
        arrived(att.at[g_of(0, e), low], ra.at[e])
        to_x(g_of(0, e), low, ra, e)
        arrived(att.at[g_of(e, 0), high], rb.at[e * NY])
        to_y(g_of(e, 0), high, rb, e)

    lanes = lax.broadcasted_iota(jnp.int32, (2 * TOK, C), 1).astype(F32)
    for dx in range(NX):
        xs = lax.rem(x + dx, NX)
        for dy in range(NY):
            g = g_of(dx, dy)
            if dx > 0:
                arrived(att.at[g, low], ra.at[dx * NY + dy])
            if dy > 0:
                arrived(att.at[g, high], rb.at[dx * NY + dy])
            col = idcol[:, pl.ds(dx * 8 + dy, 1)]
            onehot = (lanes == col).astype(F32).astype(BF16)
            picked = jnp.dot(onehot, att[g].reshape(C, E), preferred_element_type=F32)
            feat[:, pl.ds(pl.multiple_of(lax.rem(y + dy, NY) * E, E), E)] = picked.astype(BF16)
        if dx == 0:
            w_finish()
        for order in range(2):
            who = lax.rem(c + 1 + order, 2)
            rows = pl.ds(pl.multiple_of(who * TOK, TOK), TOK)

            @pl.loop(0, NX)
            def _(n):
                cols = pl.ds(pl.multiple_of(n * TOK, TOK), TOK)
                block = wbuf[pl.ds(xs * NY, NY), :, cols].reshape(NY * E, TOK)
                term = jnp.dot(feat[rows, :], block, preferred_element_type=F32)
                if dx == 0:
                    psum[rows, cols] = term
                else:
                    psum[rows, cols] += term

            if dx == NX - 1 and order == 0:
                put(psum.at[rows], other, rf.at[0], seq_of(y, z, 1 - c), x)
    arrived(other, rf.at[0])
    own = pl.ds(pl.multiple_of(c * TOK, TOK), TOK)
    out_ref[...] = (psum[own, :] + other[...]).astype(BF16)
    for cp in sends:
        cp.wait_send()
    for cond, cp in maybe:
        pl.when(cond)(cp.wait_send)


def chain(queries, keys, values, ids, idx, weight):
    vmem = pl.BlockSpec(memory_space=pltpu.VMEM)
    anyw = pl.BlockSpec(memory_space=pl.ANY)
    dma = pltpu.SemaphoreType.DMA
    return pl.pallas_call(
        chain_kernel,
        out_shape=jax.ShapeDtypeStruct((TOK, 8 * E), BF16),
        in_specs=[anyw, anyw, anyw, vmem, vmem, anyw],
        out_specs=vmem,
        scratch_shapes=[
            pltpu.VMEM((8, TOK, E), BF16), pltpu.VMEM((8, TOK, E), BF16), pltpu.VMEM((8, TOK, E), BF16),
            pltpu.VMEM((8, 1, TOK), jnp.int32), pltpu.VMEM((8, 8, TOK), jnp.int32),
            pltpu.VMEM((C, 2 * E), F32), pltpu.VMEM((2 * NZ, ROWS, E), F32),
            pltpu.VMEM((NZ - 1, ROWS, E), F32), pltpu.VMEM((NZ - 1, ROWS, E), F32),
            pltpu.VMEM((NZ, BLK, E), BF16), pltpu.VMEM((8, C, TOK), F32),
            pltpu.VMEM((C, E), F32), pltpu.VMEM((C, E), F32),
            pltpu.VMEM((16, NZ, BLK, E), BF16), pltpu.VMEM((2 * TOK, E), F32),
            pltpu.VMEM((16, E, 8 * E), BF16), pltpu.VMEM((2 * TOK, NY * E), BF16),
            pltpu.VMEM((2 * TOK, 8 * E), F32), pltpu.VMEM((TOK, 8 * E), F32),
            dma((120,)), dma((7,)), dma((7,)), dma((7,)), dma((7,)), dma((8,)), dma((7,)), dma((7,)),
            dma((7,)), dma((7,)), dma((16,)), dma((16,)), dma((4,)), dma((6,)),
            dma((8,)), dma(()), dma((4,)), dma((3,)), dma((2,)), dma((6,)),
        ],
        compiler_params=pltpu.CompilerParams(
            collective_id=0, has_side_effects=True, vmem_limit_bytes=48 * 1024 * 1024
        ),
        cost_estimate=pl.CostEstimate(flops=4_000_000_000, bytes_accessed=200_000_000, transcendentals=1 << 20),
    )(queries, keys, values, ids, idx, weight)


def on_device(queries, keys, values, cluster_ids, out_weight):
    y = lax.div(lax.axis_index("seq"), 2 * NZ)
    ids = cluster_ids.T
    pair = ids.reshape(2, NY, TOK)
    pair = lax.dynamic_slice_in_dim(jnp.concatenate([pair, pair], axis=1), y, NY, axis=1)
    idx = jnp.concatenate([pair, jnp.zeros_like(pair)], axis=1)
    q, k, v = (jnp.transpose(a, (1, 0, 2)) for a in (queries, keys, values))
    return chain(q, k, v, ids[:, None, :], idx, out_weight)


def solution(mesh):
    placed = (
        P("seq", "head", None),
        P("seq", "head", None),
        P("seq", "head", None),
        P("seq", "head"),
        P("seq", "head"),
    )
    return jax.shard_map(
        on_device, mesh=mesh, in_specs=placed, out_specs=P("seq", "head"), check_vma=False
    )
```

```python
import math

import jax
import jax.numpy as jnp
from jax import lax
from jax.experimental import pallas as pl
from jax.experimental.pallas import tpu as pltpu
from jax.sharding import PartitionSpec as P

C = 512
E = 128
NY, NZ, NX = 4, 8, 4
TOK = 256
BLK = C // NZ
HALF = E // 2
EXP2_SCALE = math.log2(math.e) / math.sqrt(E)
F32, BF16 = jnp.float32, jnp.bfloat16
SIDE = 384
SUM_T, OUT_T = BF16, BF16


def chain_kernel(
    q_ref, k_ref, v_ref, ids_ref, idx_ref, w_ref, out_ref,
    qbuf, kbuf, vbuf, idbuf, idxbuf, acc, msg_t, msg_c, msg_o, msg_m, recv_t, recv_c, recv_o, recv_m, cent, sbuf, mx, ls, oacc,
    att, idcol, wbuf, feat, psum, other,
    ssem, rq, rk, rv, rid, ridx, rt, rtc, rc, ro, rom, rz, ra, rb, rf, lsem, swc, rwo, rw1, rwr, rwl, rwy, rwa, rwra, rwla,
):
    s_id, x = lax.axis_index("seq"), lax.axis_index("head")
    c = lax.rem(s_id, 2)
    z = lax.rem(lax.div(s_id, 2), NZ)
    y = lax.div(s_id, 2 * NZ)
    yc = y * 2 + c
    g0 = x * NY + y

    def seq_of(yy, zz, cc):
        return (yy * NZ + zz) * 2 + cc

    sends = []

    def put(src, dst, rsem, seq, head):
        cp = pltpu.make_async_remote_copy(
            src_ref=src, dst_ref=dst, send_sem=ssem.at[len(sends)], recv_sem=rsem,
            device_id=(seq, head), device_id_type=pl.DeviceIdType.MESH,
        )
        cp.start()
        sends.append(cp)
        return cp

    maybe = []

    def put_if(cond, src, dst, rsem, seq, head):
        cp = pltpu.make_async_remote_copy(
            src_ref=src, dst_ref=dst, send_sem=swc.at[len(maybe)], recv_sem=rsem,
            device_id=(seq, head), device_id_type=pl.DeviceIdType.MESH,
        )
        pl.when(cond)(cp.start)
        maybe.append((cond, cp))

    def arrived(ref, rsem):
        pltpu.make_async_copy(ref, ref, rsem).wait()

    def yc_peer(d):
        t = lax.rem(yc + d, 8)
        return lax.div(t, 2), lax.rem(t, 2)

    barrier = pltpu.get_barrier_semaphore()

    def greet(seq, head):
        pl.semaphore_signal(barrier, inc=1, device_id=(seq, head), device_id_type=pl.DeviceIdType.MESH)

    for d in range(1, 8):
        ty, tc = yc_peer(d)
        greet(seq_of(ty, z, tc), x)
        greet(seq_of(y, lax.rem(z + d, NZ), c), x)
    for step in (1, NZ - 1):
        greet(seq_of(y, lax.rem(z + step, NZ), 1 - c), x)
    for e in range(1, NX):
        greet(s_id, lax.rem(x + e, NX))
        greet(seq_of(y, z, 1 - c), lax.rem(x + e, NX))

    local = []
    own_h = c * NY + y
    for n, (src, dst) in enumerate(
        ((ids_ref.at[own_h], idbuf.at[yc]), (q_ref.at[own_h], qbuf.at[yc]),
         (k_ref.at[own_h], kbuf.at[yc]), (v_ref.at[own_h], vbuf.at[yc]),
         (idx_ref.at[c], idxbuf.at[c]))
    ):
        cp = pltpu.make_async_copy(src, dst, lsem.at[n])
        cp.start()
        local.append(cp)

    pl.semaphore_wait(barrier, 22)

    for src, buf, sem in ((ids_ref, idbuf, rid), (q_ref, qbuf, rq)):
        for d in range(1, 8):
            ty, tc = yc_peer(d)
            put(src.at[tc * NY + ty], buf.at[yc], sem.at[d - 1], seq_of(ty, z, tc), x)
    put(idx_ref.at[1 - c], idxbuf.at[c], ridx.at[1], seq_of(y, z, 1 - c), x)
    for e in range(1, NX):
        for f in range(2):
            tc = lax.rem(c + f, 2)
            put(idx_ref.at[tc], idxbuf.at[(NX - e) * 2 + c], ridx.at[(NX - e) * 2 + f],
                seq_of(y, z, tc), lax.rem(x + e, NX))
    for src, buf, sem in ((k_ref, kbuf, rk), (v_ref, vbuf, rv)):
        for d in range(1, 8):
            ty, tc = yc_peer(d)
            put(src.at[tc * NY + ty], buf.at[yc], sem.at[d - 1], seq_of(ty, z, tc), x)

    home = lax.div(z, NZ // 2)
    half_rows = pl.ds(pl.multiple_of(c * HALF, HALF), HALF)
    other_rows = pl.ds(pl.multiple_of((1 - c) * HALF, HALF), HALF)

    def w_held(o):
        return lax.div(o, NZ // 2) == c

    left_cols, right_cols = pl.ds(0, SIDE), pl.ds(SIDE, 8 * E - SIDE)

    def w_b(o):
        return wbuf.at[y, lax.rem(o, NY), :, right_cols]

    def w_a(o):
        return wbuf.at[:, lax.rem(o, NY), :, left_cols]

    w_own = wbuf.at[y, lax.rem(z, NY), half_rows]
    w_copy = pltpu.make_async_copy(w_ref, w_own, lsem.at[5])
    pl.when(home == c)(w_copy.start)
    put_if(home != c, w_ref, w_own, rwo, seq_of(y, z, 1 - c), x)
    own_b = wbuf.at[y, lax.rem(z, NY), half_rows, right_cols]
    for step, sem in ((1, 0), (NZ - 1, 2)):
        put(w_ref.at[:, right_cols], own_b, rw1.at[sem + c], seq_of(y, lax.rem(z + step, NZ), home), x)

    def w_side():
        own_a = wbuf.at[y, lax.rem(z, NY), half_rows, left_cols]
        for e in range(1, NY):
            put(w_ref.at[:, left_cols], own_a, rwa.at[(e - 1) * 2 + c], seq_of(lax.rem(y + e, NY), z, home), x)

    w_side()

    def w_turn(k, far, sems, base):
        o = lax.rem(z + far * k, NZ)

        @pl.when(w_held(o))
        def _():
            if k == 1:
                for cc in range(2):
                    arrived(wbuf.at[y, lax.rem(o, NY), pl.ds(cc * HALF, HALF), right_cols], rw1.at[base + cc])
            else:
                arrived(w_b(o), sems.at[k - 2])

        return o

    def w_step(k):
        o = w_turn(k, NZ - 1, rwr, 0)
        put_if(w_held(o), w_b(o), w_b(o), rwr.at[k - 1], seq_of(y, lax.rem(z + 1, NZ), c), x)
        if k < 3:
            o = w_turn(k, 1, rwl, 2)
            put_if(w_held(o), w_b(o), w_b(o), rwl.at[k - 1], seq_of(y, lax.rem(z + NZ - 1, NZ), c), x)

    def w_spread():
        w_turn(4, NZ - 1, rwr, 0)
        w_turn(3, 1, rwl, 2)

        @pl.when(home == c)
        def _():
            w_copy.wait()
            arrived(wbuf.at[y, lax.rem(z, NY), other_rows], rwo)

        up, down = seq_of(lax.rem(y + 1, NY), z, c), seq_of(lax.rem(y + NY - 1, NY), z, c)
        for n, (lo, to) in enumerate(((0, up), (2, down), (2, up), (0, down))):
            rows = wbuf.at[y, pl.ds(lo, 2), :, right_cols]
            put(rows, rows, rwy.at[n], to, x)

    def w_relay():
        below, above = lax.rem(y + NY - 1, NY), lax.rem(y + 1, NY)
        first = wbuf.at[below, pl.ds(0, 2), :, right_cols]
        arrived(first, rwy.at[0])
        put(first, first, rwy.at[4], seq_of(above, z, c), x)
        second = wbuf.at[above, pl.ds(2, 2), :, right_cols]
        arrived(second, rwy.at[1])
        put(second, second, rwy.at[5], seq_of(below, z, c), x)

    def w_finish():
        below, above, across = lax.rem(y + NY - 1, NY), lax.rem(y + 1, NY), lax.rem(y + 2, NY)
        arrived(wbuf.at[below, pl.ds(2, 2), :, right_cols], rwy.at[2])
        arrived(wbuf.at[above, pl.ds(0, 2), :, right_cols], rwy.at[3])
        arrived(wbuf.at[across, pl.ds(0, 2), :, right_cols], rwy.at[4])
        arrived(wbuf.at[across, pl.ds(2, 2), :, right_cols], rwy.at[5])
        a_wait(4, NZ - 1, rwra)
        a_wait(3, 1, rwla)

    def a_wait(k, far, sems):
        o = lax.rem(z + far * k, NZ)

        @pl.when(w_held(o))
        def _():
            arrived(w_a(o), sems.at[k - 1])

    def a_step(k):
        if k == 0:
            @pl.when(home == c)
            def _():
                for e in range(1, NY):
                    for cc in range(2):
                        arrived(wbuf.at[lax.rem(y + NY - e, NY), lax.rem(z, NY), pl.ds(cc * HALF, HALF), left_cols],
                                rwa.at[(e - 1) * 2 + cc])
        else:
            a_wait(k, NZ - 1, rwra)
            if k < 3:
                a_wait(k, 1, rwla)
        o = lax.rem(z + (NZ - 1) * k, NZ)
        put_if(w_held(o), w_a(o), w_a(o), rwra.at[k], seq_of(y, lax.rem(z + 1, NZ), c), x)
        if k < 3:
            o = lax.rem(z + k, NZ)
            put_if(w_held(o), w_a(o), w_a(o), rwla.at[k], seq_of(y, lax.rem(z + NZ - 1, NZ), c), x)

    def take8(buf, sem):
        for d in range(1, 8):
            arrived(buf.at[lax.rem(yc + 8 - d, 8)], sem.at[d - 1])

    eye = lax.broadcasted_iota(jnp.int32, (BLK, E), 0) == lax.broadcasted_iota(jnp.int32, (BLK, E), 1)

    def to_row(col):
        return jnp.sum(jnp.where(eye, col, 0.0), axis=0, keepdims=True)

    def to_col(row):
        return jnp.sum(jnp.where(eye, row, 0.0), axis=1, keepdims=True)

    local[0].wait()
    local[1].wait()
    acc[...] = jnp.zeros_like(acc)

    @pl.loop(0, 8)
    def _(d):
        i = lax.rem(yc + 8 - d, 8)

        @pl.when(d > 0)
        def _():
            arrived(idbuf.at[i], rid.at[d - 1])
            arrived(qbuf.at[i], rq.at[d - 1])

        label = lax.broadcasted_iota(jnp.int32, (C, TOK), 0)
        onehot = (label == idbuf[i]).astype(F32).astype(BF16)
        rhs = jnp.concatenate([qbuf[i], jnp.ones((TOK, E), BF16)], axis=1)
        acc[...] += jnp.dot(onehot, rhs, preferred_element_type=F32)

    @pl.loop(0, NZ)
    def _(b):
        rows = pl.ds(pl.multiple_of(b * BLK, BLK), BLK)
        msg_t[b] = acc[rows, pl.ds(0, E)].astype(SUM_T)
        msg_c[b] = jnp.broadcast_to(to_row(acc[rows, pl.ds(E, E)]), (8, E))

    for d in (4, 3, 5, 2, 6, 1, 7):
        tz = lax.rem(z + d, NZ)
        put(msg_c.at[tz], recv_c.at[d - 1], rtc.at[d - 1], seq_of(y, tz, c), x)
        put(msg_t.at[tz], recv_t.at[d - 1], rt.at[d - 1], seq_of(y, tz, c), x)
    w_step(1)

    local[4].wait()
    for j in range(1, 8):
        e, f = j // 2, j % 2
        arrived(idxbuf.at[e * 2 + lax.rem(c + f, 2)], ridx.at[j])
    for half in range(2):
        rows = jnp.concatenate([idxbuf[e * 2 + half] for e in range(NX)], axis=0).astype(F32)
        rows = jnp.concatenate([rows, jnp.zeros((E - 8 * NX, TOK), F32)], axis=0)
        idcol[pl.ds(half * TOK, TOK), :] = rows.T

    w_step(2)
    total, count = msg_t[z].astype(F32), msg_c[z]
    for d in range(1, NZ):
        arrived(recv_c.at[d - 1], rtc.at[d - 1])
        arrived(recv_t.at[d - 1], rt.at[d - 1])
        total = total + recv_t[d - 1].astype(F32)
        count = count + recv_c[d - 1]
    count = to_col(count[:1])
    cent[z] = (total / jnp.maximum(count, 1.0)).astype(BF16)

    for d in (4, 3, 5, 2, 6, 1, 7):
        tz = lax.rem(z + d, NZ)
        put(cent.at[z], cent.at[z], rc.at[d - 1], seq_of(y, tz, c), x)
    w_step(3)
    local[2].wait()
    take8(kbuf, rk)
    for d in range(1, NZ):
        arrived(cent.at[lax.rem(z + NZ - d, NZ)], rc.at[d - 1])

    w_spread()
    a_step(0)
    half = C // 2
    for part, dist in enumerate(((4, 3, 5, 2), (6, 1, 7, 0))):
        centroid = jnp.concatenate([cent[lax.rem(z + d, NZ)] for d in dist], axis=0)
        mx[...] = jnp.full_like(mx, -jnp.inf)

        @pl.loop(0, 8)
        def _(i):
            s = lax.dot_general(centroid, kbuf[i], (((1,), (1,)), ((), ())), preferred_element_type=F32)
            sbuf[i] = s
            mx[...] = jnp.maximum(mx[...], jnp.maximum(s[:, :E], s[:, E:]))

        mx[...] = jnp.broadcast_to(jnp.max(mx[...], axis=1, keepdims=True), (half, E))
        ls[...] = jnp.zeros_like(ls)
        if part == 0:
            local[3].wait()
            take8(vbuf, rv)
        oacc[...] = jnp.zeros_like(oacc)

        @pl.loop(0, 8)
        def _(i):
            m = mx[...]
            p = jnp.exp2((sbuf[i] - jnp.concatenate([m, m], axis=1)) * EXP2_SCALE)
            ls[...] += p[:, :E] + p[:, E:]
            oacc[...] += jnp.dot(p.astype(BF16), vbuf[i], preferred_element_type=F32)

        ls[...] = jnp.broadcast_to(jnp.sum(ls[...], axis=1, keepdims=True), (half, E))
        first = lax.broadcasted_iota(jnp.int32, (8, E), 0) == 0
        for j, d in enumerate(dist):
            rows = pl.ds(j * BLK, BLK)
            msg_m[d] = jnp.where(first, to_row(mx[rows, :]), to_row(ls[rows, :]))
            msg_o[d] = oacc[rows, :].astype(OUT_T)
            if d > 0:
                tz = lax.rem(z + d, NZ)
                put(msg_m.at[d], recv_m.at[d - 1], rom.at[d - 1], seq_of(y, tz, c), x)
                put(msg_o.at[d], recv_o.at[d - 1], ro.at[d - 1], seq_of(y, tz, c), x)

    a_step(1)
    stats, parts = [msg_m[0]], [msg_o[0]]
    for d in range(1, NZ):
        arrived(recv_m.at[d - 1], rom.at[d - 1])
        arrived(recv_o.at[d - 1], ro.at[d - 1])
        stats.append(recv_m[d - 1])
        parts.append(recv_o[d - 1])
    tops = [to_col(stat[:1]) for stat in stats]
    largest = tops[0]
    for t in tops[1:]:
        largest = jnp.maximum(largest, t)
    num, den = 0.0, 0.0
    for stat, part, t in zip(stats, parts, tops):
        factor = jnp.exp2((t - largest) * EXP2_SCALE)
        num = num + part.astype(F32) * factor
        den = den + to_col(stat[1:2]) * factor
    att[g0, z] = (num / den).astype(BF16)

    for d in (4, 3, 5, 2, 6, 1, 7):
        tz = lax.rem(z + d, NZ)
        put(att.at[g0, z], att.at[g0, z], rz.at[d - 1], seq_of(y, tz, c), x)
    w_relay()
    a_step(2)
    for d in range(1, NZ):
        arrived(att.at[g0, lax.rem(z + NZ - d, NZ)], rz.at[d - 1])

    a_step(3)
    low, high = pl.ds(0, NZ // 2), pl.ds(NZ // 2, NZ // 2)

    def g_of(dx, dy):
        return lax.rem(x + dx, NX) * NY + lax.rem(y + dy, NY)

    def to_y(g, part, sem, dx):
        for e in range(1, NY):
            put(att.at[g, part], att.at[g, part], sem.at[dx * NY + NY - e],
                seq_of(lax.rem(y + e, NY), z, c), x)

    def to_x(g, part, sem, dy):
        for e in range(1, NX):
            put(att.at[g, part], att.at[g, part], sem.at[(NX - e) * NY + dy],
                s_id, lax.rem(x + e, NX))

    to_y(g0, low, ra, 0)
    to_x(g0, high, rb, 0)
    to_x(g0, low, ra, 0)
    to_y(g0, high, rb, 0)
    for e in range(1, NY):
        arrived(att.at[g_of(0, e), low], ra.at[e])
        to_x(g_of(0, e), low, ra, e)
        arrived(att.at[g_of(e, 0), high], rb.at[e * NY])
        to_y(g_of(e, 0), high, rb, e)

    lanes = lax.broadcasted_iota(jnp.int32, (2 * TOK, C), 1).astype(F32)
    groups = (
        ((0, 0), (0, 1), (0, 2), (0, 3)),
        ((1, 0), (2, 0), (3, 0)),
        ((1, 1), (1, 2), (2, 1), (2, 2)),
        ((1, 3), (3, 1), (2, 3), (3, 2), (3, 3)),
    )
    mine = pl.ds(pl.multiple_of(c * TOK, TOK), TOK)
    theirs = pl.ds(pl.multiple_of((1 - c) * TOK, TOK), TOK)
    for at, heads in enumerate(groups):
        for n, (dx, dy) in enumerate(heads):
            g = g_of(dx, dy)
            if dx > 0:
                arrived(att.at[g, low], ra.at[dx * NY + dy])
            if dy > 0:
                arrived(att.at[g, high], rb.at[dx * NY + dy])
            col = idcol[:, pl.ds(dx * 8 + dy, 1)]
            onehot = (lanes == col).astype(F32).astype(BF16)
            picked = jnp.dot(onehot, att[g].reshape(C, E), preferred_element_type=F32)
            feat[:, pl.ds(n * E, E)] = picked.astype(BF16)
        if at == 0:
            w_finish()

        def term(rows, cols):
            block = jnp.concatenate(
                [wbuf[lax.rem(x + dx, NX), lax.rem(y + dy, NY), :, cols] for dx, dy in heads], axis=0
            )
            return jnp.dot(feat[rows, pl.ds(0, len(heads) * E)], block, preferred_element_type=F32)

        if at < len(groups) - 1:
            @pl.loop(0, NX)
            def _(n):
                cols = pl.ds(pl.multiple_of(n * TOK, TOK), TOK)
                if at == 0:
                    psum[:, cols] = term(slice(None), cols)
                else:
                    psum[:, cols] += term(slice(None), cols)
        else:
            for n in range(NX):
                cols = pl.ds(n * TOK, TOK)
                psum[theirs, cols] += term(theirs, cols)
                put(psum.at[theirs, cols], other.at[:, cols], rf.at[n], seq_of(y, z, 1 - c), x)
            for n in range(NX):
                cols = pl.ds(n * TOK, TOK)
                total = psum[mine, cols] + term(mine, cols)
                arrived(other.at[:, cols], rf.at[n])
                out_ref[:, cols] = (total + other[:, cols]).astype(BF16)
    for cp in sends:
        cp.wait_send()
    for cond, cp in maybe:
        pl.when(cond)(cp.wait_send)


def chain(queries, keys, values, ids, idx, weight):
    vmem = pl.BlockSpec(memory_space=pltpu.VMEM)
    anyw = pl.BlockSpec(memory_space=pl.ANY)
    dma = pltpu.SemaphoreType.DMA
    return pl.pallas_call(
        chain_kernel,
        out_shape=jax.ShapeDtypeStruct((TOK, 8 * E), BF16),
        in_specs=[anyw, anyw, anyw, vmem, vmem, anyw],
        out_specs=vmem,
        scratch_shapes=[
            pltpu.VMEM((8, TOK, E), BF16), pltpu.VMEM((8, TOK, E), BF16), pltpu.VMEM((8, TOK, E), BF16),
            pltpu.VMEM((8, 1, TOK), jnp.int32), pltpu.VMEM((8, 8, TOK), jnp.int32),
            pltpu.VMEM((C, 2 * E), F32),
            pltpu.VMEM((NZ, BLK, E), SUM_T), pltpu.VMEM((NZ, 8, E), F32),
            pltpu.VMEM((NZ, BLK, E), OUT_T), pltpu.VMEM((NZ, 8, E), F32),
            pltpu.VMEM((NZ - 1, BLK, E), SUM_T), pltpu.VMEM((NZ - 1, 8, E), F32),
            pltpu.VMEM((NZ - 1, BLK, E), OUT_T), pltpu.VMEM((NZ - 1, 8, E), F32),
            pltpu.VMEM((NZ, BLK, E), BF16), pltpu.VMEM((8, C // 2, TOK), F32),
            pltpu.VMEM((C // 2, E), F32), pltpu.VMEM((C // 2, E), F32), pltpu.VMEM((C // 2, E), F32),
            pltpu.VMEM((16, NZ, BLK, E), BF16), pltpu.VMEM((2 * TOK, E), F32),
            pltpu.VMEM((NX, NY, E, 8 * E), BF16), pltpu.VMEM((2 * TOK, 5 * E), BF16),
            pltpu.VMEM((2 * TOK, 8 * E), F32), pltpu.VMEM((TOK, 8 * E), F32),
            dma((144,)), dma((7,)), dma((7,)), dma((7,)), dma((7,)), dma((8,)),
            dma((7,)), dma((7,)), dma((7,)), dma((7,)), dma((7,)), dma((7,)),
            dma((16,)), dma((16,)), dma((4,)), dma((6,)),
            dma((16,)), dma(()), dma((4,)), dma((3,)), dma((2,)), dma((6,)), dma((6,)), dma((4,)), dma((3,)),
        ],
        compiler_params=pltpu.CompilerParams(
            collective_id=0, has_side_effects=True, vmem_limit_bytes=48 * 1024 * 1024
        ),
        cost_estimate=pl.CostEstimate(flops=4_000_000_000, bytes_accessed=200_000_000, transcendentals=1 << 20),
    )(queries, keys, values, ids, idx, weight)


def on_device(queries, keys, values, cluster_ids, out_weight):
    y = lax.div(lax.axis_index("seq"), 2 * NZ)
    ids = cluster_ids.T
    pair = ids.reshape(2, NY, TOK)
    pair = lax.dynamic_slice_in_dim(jnp.concatenate([pair, pair], axis=1), y, NY, axis=1)
    idx = jnp.concatenate([pair, jnp.zeros_like(pair)], axis=1)
    q, k, v = (jnp.transpose(a, (1, 0, 2)) for a in (queries, keys, values))
    return chain(q, k, v, ids[:, None, :], idx, out_weight)


def solution(mesh):
    placed = (
        P("seq", "head", None),
        P("seq", "head", None),
        P("seq", "head", None),
        P("seq", "head"),
        P("seq", "head"),
    )
    return jax.shard_map(
        on_device, mesh=mesh, in_specs=placed, out_specs=P("seq", "head"), check_vma=False
    )
```

```python
import math

import jax
import jax.numpy as jnp
from jax import lax
from jax.experimental import pallas as pl
from jax.experimental.pallas import tpu as pltpu
from jax.sharding import PartitionSpec as P

C = 512
E = 128
NY, NZ, NX = 4, 8, 4
TOK = 256
BLK = C // NZ
HALF = E // 2
EXP2_SCALE = math.log2(math.e) / math.sqrt(E)
F32, BF16 = jnp.float32, jnp.bfloat16
SIDE = 256
SUM_T, OUT_T = BF16, BF16


def chain_kernel(
    q_ref, k_ref, v_ref, ids_ref, w_ref, out_ref,
    qbuf, kbuf, vbuf, idst, idbuf, idxbuf, acc, msg_t, msg_c, msg_o, msg_m, recv_t, recv_c, recv_o, recv_m, cent, sbuf, mx, ls, oacc,
    att, idrow, idcol, wbuf, feat, psum, other,
    ssem, rq, rk, rv, rid, ridx, rt, rtc, rc, ro, rom, rz, ra, rb, rf, lsem, swc, rwo, rw1, rwr, rwl, rwy, rwa, rwra, rwla, zup, zdown,
):
    s_id, x = lax.axis_index("seq"), lax.axis_index("head")
    c = lax.rem(s_id, 2)
    z = lax.rem(lax.div(s_id, 2), NZ)
    y = lax.div(s_id, 2 * NZ)
    yc = y * 2 + c
    g0 = x * NY + y

    def seq_of(yy, zz, cc):
        return (yy * NZ + zz) * 2 + cc

    sends = []

    def put(src, dst, rsem, seq, head):
        cp = pltpu.make_async_remote_copy(
            src_ref=src, dst_ref=dst, send_sem=ssem.at[len(sends)], recv_sem=rsem,
            device_id=(seq, head), device_id_type=pl.DeviceIdType.MESH,
        )
        cp.start()
        sends.append(cp)
        return cp

    maybe = []

    def put_if(cond, src, dst, rsem, seq, head):
        cp = pltpu.make_async_remote_copy(
            src_ref=src, dst_ref=dst, send_sem=swc.at[len(maybe)], recv_sem=rsem,
            device_id=(seq, head), device_id_type=pl.DeviceIdType.MESH,
        )
        pl.when(cond)(cp.start)
        maybe.append((cond, cp))

    def arrived(ref, rsem):
        pltpu.make_async_copy(ref, ref, rsem).wait()

    def yc_peer(d):
        t = lax.rem(yc + d, 8)
        return lax.div(t, 2), lax.rem(t, 2)

    barrier = pltpu.get_barrier_semaphore()

    def greet(seq, head):
        pl.semaphore_signal(barrier, inc=1, device_id=(seq, head), device_id_type=pl.DeviceIdType.MESH)

    for d in range(1, 8):
        ty, tc = yc_peer(d)
        greet(seq_of(ty, z, tc), x)
    for step in (1, NZ - 1):
        greet(seq_of(y, lax.rem(z + step, NZ), 0), x)
        greet(seq_of(y, lax.rem(z + step, NZ), 1), x)
    for e in range(1, NX):
        greet(s_id, lax.rem(x + e, NX))
        greet(seq_of(y, z, 1 - c), lax.rem(x + e, NX))

    for h in range(8):
        idst[h] = ids_ref[pl.ds(h, 1), :]
    local = []
    own_h = c * NY + y
    for n, (src, dst) in enumerate(
        ((idst.at[own_h], idbuf.at[yc]), (q_ref.at[own_h], qbuf.at[yc]),
         (k_ref.at[own_h], kbuf.at[yc]), (v_ref.at[own_h], vbuf.at[yc]),
         (ids_ref, idxbuf.at[c]))
    ):
        cp = pltpu.make_async_copy(src, dst, lsem.at[n])
        cp.start()
        local.append(cp)

    pl.semaphore_wait(barrier, 17)

    for d in range(1, 8):
        ty, tc = yc_peer(d)
        put(idst.at[tc * NY + ty], idbuf.at[yc], rid.at[d - 1], seq_of(ty, z, tc), x)
    for d in range(1, 8):
        ty, tc = yc_peer(d)
        put(q_ref.at[tc * NY + ty], qbuf.at[yc], rq.at[d - 1], seq_of(ty, z, tc), x)
    put(ids_ref, idxbuf.at[c], ridx.at[1], seq_of(y, z, 1 - c), x)
    for e in range(1, NX):
        for f in range(2):
            tc = lax.rem(c + f, 2)
            put(ids_ref, idxbuf.at[(NX - e) * 2 + c], ridx.at[(NX - e) * 2 + f],
                seq_of(y, z, tc), lax.rem(x + e, NX))
    for src, buf, sem in ((k_ref, kbuf, rk), (v_ref, vbuf, rv)):
        for d in range(1, 8):
            ty, tc = yc_peer(d)
            put(src.at[tc * NY + ty], buf.at[yc], sem.at[d - 1], seq_of(ty, z, tc), x)

    home = lax.div(z, NZ // 2)
    half_rows = pl.ds(pl.multiple_of(c * HALF, HALF), HALF)
    other_rows = pl.ds(pl.multiple_of((1 - c) * HALF, HALF), HALF)

    def w_held(o):
        return lax.div(o, NZ // 2) == c

    left_cols, right_cols = pl.ds(0, SIDE), pl.ds(SIDE, 8 * E - SIDE)

    def w_b(o):
        return wbuf.at[y, lax.rem(o, NY), :, right_cols]

    def w_a(o):
        return wbuf.at[:, lax.rem(o, NY), :, left_cols]

    w_own = wbuf.at[y, lax.rem(z, NY), half_rows]
    w_copy = pltpu.make_async_copy(w_ref, w_own, lsem.at[5])
    pl.when(home == c)(w_copy.start)
    put_if(home != c, w_ref, w_own, rwo, seq_of(y, z, 1 - c), x)
    own_b = wbuf.at[y, lax.rem(z, NY), half_rows, right_cols]
    for step, sem in ((1, 0), (NZ - 1, 2)):
        put(w_ref.at[:, right_cols], own_b, rw1.at[sem + c], seq_of(y, lax.rem(z + step, NZ), home), x)

    def w_side():
        own_a = wbuf.at[y, lax.rem(z, NY), half_rows, left_cols]
        for e in range(1, NY):
            put(w_ref.at[:, left_cols], own_a, rwa.at[(e - 1) * 2 + c], seq_of(lax.rem(y + e, NY), z, home), x)

    w_side()

    def w_turn(k, far, sems, base):
        o = lax.rem(z + far * k, NZ)

        @pl.when(w_held(o))
        def _():
            if k == 1:
                for cc in range(2):
                    arrived(wbuf.at[y, lax.rem(o, NY), pl.ds(cc * HALF, HALF), right_cols], rw1.at[base + cc])
            else:
                arrived(w_b(o), sems.at[k - 2])

        return o

    def w_step(k):
        o = w_turn(k, NZ - 1, rwr, 0)
        put_if(w_held(o), w_b(o), w_b(o), rwr.at[k - 1], seq_of(y, lax.rem(z + 1, NZ), c), x)
        if k < 3:
            o = w_turn(k, 1, rwl, 2)
            put_if(w_held(o), w_b(o), w_b(o), rwl.at[k - 1], seq_of(y, lax.rem(z + NZ - 1, NZ), c), x)

    def w_spread():
        w_turn(4, NZ - 1, rwr, 0)
        w_turn(3, 1, rwl, 2)

        @pl.when(home == c)
        def _():
            w_copy.wait()
            arrived(wbuf.at[y, lax.rem(z, NY), other_rows], rwo)

        up, down = seq_of(lax.rem(y + 1, NY), z, c), seq_of(lax.rem(y + NY - 1, NY), z, c)
        for n, (lo, to) in enumerate(((0, up), (2, down), (2, up), (0, down))):
            rows = wbuf.at[y, pl.ds(lo, 2), :, right_cols]
            put(rows, rows, rwy.at[n], to, x)

    def w_relay():
        below, above = lax.rem(y + NY - 1, NY), lax.rem(y + 1, NY)
        first = wbuf.at[below, pl.ds(0, 2), :, right_cols]
        arrived(first, rwy.at[0])
        put(first, first, rwy.at[4], seq_of(above, z, c), x)
        second = wbuf.at[above, pl.ds(2, 2), :, right_cols]
        arrived(second, rwy.at[1])
        put(second, second, rwy.at[5], seq_of(below, z, c), x)

    def w_finish():
        below, above, across = lax.rem(y + NY - 1, NY), lax.rem(y + 1, NY), lax.rem(y + 2, NY)
        arrived(wbuf.at[below, pl.ds(2, 2), :, right_cols], rwy.at[2])
        arrived(wbuf.at[above, pl.ds(0, 2), :, right_cols], rwy.at[3])
        arrived(wbuf.at[across, pl.ds(0, 2), :, right_cols], rwy.at[4])
        arrived(wbuf.at[across, pl.ds(2, 2), :, right_cols], rwy.at[5])
        a_wait(4, NZ - 1, rwra)
        a_wait(3, 1, rwla)

    def a_wait(k, far, sems):
        o = lax.rem(z + far * k, NZ)

        @pl.when(w_held(o))
        def _():
            arrived(w_a(o), sems.at[k - 1])

    def a_step(k):
        if k == 0:
            @pl.when(home == c)
            def _():
                for e in range(1, NY):
                    for cc in range(2):
                        arrived(wbuf.at[lax.rem(y + NY - e, NY), lax.rem(z, NY), pl.ds(cc * HALF, HALF), left_cols],
                                rwa.at[(e - 1) * 2 + cc])
        else:
            a_wait(k, NZ - 1, rwra)
            if k < 3:
                a_wait(k, 1, rwla)
        o = lax.rem(z + (NZ - 1) * k, NZ)
        put_if(w_held(o), w_a(o), w_a(o), rwra.at[k], seq_of(y, lax.rem(z + 1, NZ), c), x)
        if k < 3:
            o = lax.rem(z + k, NZ)
            put_if(w_held(o), w_a(o), w_a(o), rwla.at[k], seq_of(y, lax.rem(z + NZ - 1, NZ), c), x)

    def take8(buf, sem):
        for d in range(1, 8):
            arrived(buf.at[lax.rem(yc + 8 - d, 8)], sem.at[d - 1])

    eye = lax.broadcasted_iota(jnp.int32, (BLK, E), 0) == lax.broadcasted_iota(jnp.int32, (BLK, E), 1)

    def to_row(col):
        return jnp.sum(jnp.where(eye, col, 0.0), axis=0, keepdims=True)

    def to_col(row):
        return jnp.sum(jnp.where(eye, row, 0.0), axis=1, keepdims=True)

    local[0].wait()
    local[1].wait()
    acc[...] = jnp.zeros_like(acc)
    for k in range(3):
        pl.semaphore_signal(zup, inc=1, device_id=(seq_of(y, lax.rem(z + 1, NZ), c), x), device_id_type=pl.DeviceIdType.MESH)
        if k < 2:
            pl.semaphore_signal(zdown, inc=1, device_id=(seq_of(y, lax.rem(z + NZ - 1, NZ), c), x), device_id_type=pl.DeviceIdType.MESH)
            pl.semaphore_wait(zdown, 1)
        pl.semaphore_wait(zup, 1)
    w_step(1)

    @pl.loop(0, 8)
    def _(d):
        i = lax.rem(yc + 8 - d, 8)

        @pl.when(d > 0)
        def _():
            arrived(idbuf.at[i], rid.at[d - 1])
            arrived(qbuf.at[i], rq.at[d - 1])

        label = lax.broadcasted_iota(jnp.int32, (C, TOK), 0)
        onehot = (label == idbuf[i]).astype(F32).astype(BF16)
        rhs = jnp.concatenate([qbuf[i], jnp.ones((TOK, E), BF16)], axis=1)
        acc[...] += jnp.dot(onehot, rhs, preferred_element_type=F32)

    @pl.loop(0, NZ)
    def _(b):
        rows = pl.ds(pl.multiple_of(b * BLK, BLK), BLK)
        msg_t[b] = acc[rows, pl.ds(0, E)].astype(SUM_T)
        msg_c[b] = jnp.broadcast_to(to_row(acc[rows, pl.ds(E, E)]), (8, E))

    for d in (4, 3, 5, 2, 6, 1, 7):
        tz = lax.rem(z + d, NZ)
        put(msg_c.at[tz], recv_c.at[d - 1], rtc.at[d - 1], seq_of(y, tz, c), x)
        put(msg_t.at[tz], recv_t.at[d - 1], rt.at[d - 1], seq_of(y, tz, c), x)

    w_step(2)
    local[4].wait()
    for j in range(1, 8):
        e, f = j // 2, j % 2
        arrived(idxbuf.at[e * 2 + lax.rem(c + f, 2)], ridx.at[j])
    idrow[...] = jnp.zeros_like(idrow)
    for e in range(NX):
        for dy in range(NY):
            for part in range(2):
                row = idxbuf[e * 2 + part, pl.ds(c * NY + lax.rem(y + dy, NY), 1), :]
                idrow[pl.ds(e * 8 + dy, 1), pl.ds(part * TOK, TOK)] = row.astype(F32)
    idcol[...] = idrow[...].T

    w_step(3)
    total, count = msg_t[z].astype(F32), msg_c[z]
    for d in range(1, NZ):
        arrived(recv_c.at[d - 1], rtc.at[d - 1])
        arrived(recv_t.at[d - 1], rt.at[d - 1])
        total = total + recv_t[d - 1].astype(F32)
        count = count + recv_c[d - 1]
    count = to_col(count[:1])
    cent[z] = (total / jnp.maximum(count, 1.0)).astype(BF16)

    for d in (4, 3, 5, 2, 6, 1, 7):
        tz = lax.rem(z + d, NZ)
        put(cent.at[z], cent.at[z], rc.at[d - 1], seq_of(y, tz, c), x)
    w_spread()
    local[2].wait()
    take8(kbuf, rk)
    for d in range(1, NZ):
        arrived(cent.at[lax.rem(z + NZ - d, NZ)], rc.at[d - 1])

    a_step(0)
    half = C // 2
    for part, dist in enumerate(((4, 3, 5, 2), (6, 1, 7, 0))):
        centroid = jnp.concatenate([cent[lax.rem(z + d, NZ)] for d in dist], axis=0)
        mx[...] = jnp.full_like(mx, -jnp.inf)

        @pl.loop(0, 8)
        def _(i):
            s = lax.dot_general(centroid, kbuf[i], (((1,), (1,)), ((), ())), preferred_element_type=F32)
            sbuf[i] = s
            mx[...] = jnp.maximum(mx[...], jnp.maximum(s[:, :E], s[:, E:]))

        mx[...] = jnp.broadcast_to(jnp.max(mx[...], axis=1, keepdims=True), (half, E))
        ls[...] = jnp.zeros_like(ls)
        if part == 0:
            local[3].wait()
            take8(vbuf, rv)
        oacc[...] = jnp.zeros_like(oacc)

        @pl.loop(0, 8)
        def _(i):
            m = mx[...]
            p = jnp.exp2((sbuf[i] - jnp.concatenate([m, m], axis=1)) * EXP2_SCALE)
            ls[...] += p[:, :E] + p[:, E:]
            oacc[...] += jnp.dot(p.astype(BF16), vbuf[i], preferred_element_type=F32)

        ls[...] = jnp.broadcast_to(jnp.sum(ls[...], axis=1, keepdims=True), (half, E))
        first = lax.broadcasted_iota(jnp.int32, (8, E), 0) == 0
        for j, d in enumerate(dist):
            rows = pl.ds(j * BLK, BLK)
            msg_m[d] = jnp.where(first, to_row(mx[rows, :]), to_row(ls[rows, :]))
            msg_o[d] = oacc[rows, :].astype(OUT_T)
            if d > 0:
                tz = lax.rem(z + d, NZ)
                put(msg_m.at[d], recv_m.at[d - 1], rom.at[d - 1], seq_of(y, tz, c), x)
                put(msg_o.at[d], recv_o.at[d - 1], ro.at[d - 1], seq_of(y, tz, c), x)

    a_step(1)
    w_relay()
    stats, parts = [msg_m[0]], [msg_o[0]]
    for d in range(1, NZ):
        arrived(recv_m.at[d - 1], rom.at[d - 1])
        arrived(recv_o.at[d - 1], ro.at[d - 1])
        stats.append(recv_m[d - 1])
        parts.append(recv_o[d - 1])
    tops = [to_col(stat[:1]) for stat in stats]
    largest = tops[0]
    for t in tops[1:]:
        largest = jnp.maximum(largest, t)
    num, den = 0.0, 0.0
    for stat, part, t in zip(stats, parts, tops):
        factor = jnp.exp2((t - largest) * EXP2_SCALE)
        num = num + part.astype(F32) * factor
        den = den + to_col(stat[1:2]) * factor
    att[g0, z] = (num / den).astype(BF16)

    for d in (4, 3, 5, 2, 6, 1, 7):
        tz = lax.rem(z + d, NZ)
        put(att.at[g0, z], att.at[g0, z], rz.at[d - 1], seq_of(y, tz, c), x)
    a_step(2)
    for d in range(1, NZ):
        arrived(att.at[g0, lax.rem(z + NZ - d, NZ)], rz.at[d - 1])

    a_step(3)
    low, high = pl.ds(0, NZ // 2), pl.ds(NZ // 2, NZ // 2)

    def g_of(dx, dy):
        return lax.rem(x + dx, NX) * NY + lax.rem(y + dy, NY)

    def to_y(g, part, sem, dx):
        for e in range(1, NY):
            put(att.at[g, part], att.at[g, part], sem.at[dx * NY + NY - e],
                seq_of(lax.rem(y + e, NY), z, c), x)

    def to_x(g, part, sem, dy):
        for e in range(1, NX):
            put(att.at[g, part], att.at[g, part], sem.at[(NX - e) * NY + dy],
                s_id, lax.rem(x + e, NX))

    to_y(g0, low, ra, 0)
    to_x(g0, high, rb, 0)
    to_x(g0, low, ra, 0)
    to_y(g0, high, rb, 0)
    for e in range(1, NY):
        arrived(att.at[g_of(0, e), low], ra.at[e])
        to_x(g_of(0, e), low, ra, e)
        arrived(att.at[g_of(e, 0), high], rb.at[e * NY])
        to_y(g_of(e, 0), high, rb, e)

    lanes = lax.broadcasted_iota(jnp.int32, (2 * TOK, C), 1).astype(F32)
    groups = (
        ((0, 0), (0, 1), (0, 2), (0, 3)),
        ((1, 0), (2, 0), (3, 0)),
        ((1, 1), (1, 2), (2, 1), (2, 2)),
        ((1, 3), (3, 1), (2, 3), (3, 2), (3, 3)),
    )
    mine = pl.ds(pl.multiple_of(c * TOK, TOK), TOK)
    theirs = pl.ds(pl.multiple_of((1 - c) * TOK, TOK), TOK)
    for at, heads in enumerate(groups):
        for n, (dx, dy) in enumerate(heads):
            g = g_of(dx, dy)
            if dx > 0:
                arrived(att.at[g, low], ra.at[dx * NY + dy])
            if dy > 0:
                arrived(att.at[g, high], rb.at[dx * NY + dy])
            col = idcol[:, pl.ds(dx * 8 + dy, 1)]
            onehot = (lanes == col).astype(F32).astype(BF16)
            picked = jnp.dot(onehot, att[g].reshape(C, E), preferred_element_type=F32)
            feat[:, pl.ds(n * E, E)] = picked.astype(BF16)
        if at == 0:
            w_finish()

        def term(rows, cols):
            block = jnp.concatenate(
                [wbuf[lax.rem(x + dx, NX), lax.rem(y + dy, NY), :, cols] for dx, dy in heads], axis=0
            )
            return jnp.dot(feat[rows, pl.ds(0, len(heads) * E)], block, preferred_element_type=F32)

        if at < len(groups) - 1:
            @pl.loop(0, NX)
            def _(n):
                cols = pl.ds(pl.multiple_of(n * TOK, TOK), TOK)
                if at == 0:
                    psum[:, cols] = term(slice(None), cols)
                else:
                    psum[:, cols] += term(slice(None), cols)
        else:
            for n in range(NX):
                cols = pl.ds(n * TOK, TOK)
                psum[theirs, cols] += term(theirs, cols)
                put(psum.at[theirs, cols], other.at[:, cols], rf.at[n], seq_of(y, z, 1 - c), x)
            for n in range(NX):
                cols = pl.ds(n * TOK, TOK)
                total = psum[mine, cols] + term(mine, cols)
                arrived(other.at[:, cols], rf.at[n])
                out_ref[:, cols] = (total + other[:, cols]).astype(BF16)
    for cp in sends:
        cp.wait_send()
    for cond, cp in maybe:
        pl.when(cond)(cp.wait_send)


def chain(queries, keys, values, ids, weight):
    vmem = pl.BlockSpec(memory_space=pltpu.VMEM)
    anyw = pl.BlockSpec(memory_space=pl.ANY)
    dma = pltpu.SemaphoreType.DMA
    return pl.pallas_call(
        chain_kernel,
        out_shape=jax.ShapeDtypeStruct((TOK, 8 * E), BF16),
        in_specs=[anyw, anyw, anyw, vmem, anyw],
        out_specs=vmem,
        scratch_shapes=[
            pltpu.VMEM((8, TOK, E), BF16), pltpu.VMEM((8, TOK, E), BF16), pltpu.VMEM((8, TOK, E), BF16),
            pltpu.VMEM((8, 1, TOK), jnp.int32), pltpu.VMEM((8, 1, TOK), jnp.int32), pltpu.VMEM((8, 8, TOK), jnp.int32),
            pltpu.VMEM((C, 2 * E), F32),
            pltpu.VMEM((NZ, BLK, E), SUM_T), pltpu.VMEM((NZ, 8, E), F32),
            pltpu.VMEM((NZ, BLK, E), OUT_T), pltpu.VMEM((NZ, 8, E), F32),
            pltpu.VMEM((NZ - 1, BLK, E), SUM_T), pltpu.VMEM((NZ - 1, 8, E), F32),
            pltpu.VMEM((NZ - 1, BLK, E), OUT_T), pltpu.VMEM((NZ - 1, 8, E), F32),
            pltpu.VMEM((NZ, BLK, E), BF16), pltpu.VMEM((8, C // 2, TOK), F32),
            pltpu.VMEM((C // 2, E), F32), pltpu.VMEM((C // 2, E), F32), pltpu.VMEM((C // 2, E), F32),
            pltpu.VMEM((16, NZ, BLK, E), BF16), pltpu.VMEM((E, 2 * TOK), F32), pltpu.VMEM((2 * TOK, E), F32),
            pltpu.VMEM((NX, NY, E, 8 * E), BF16), pltpu.VMEM((2 * TOK, 5 * E), BF16),
            pltpu.VMEM((2 * TOK, 8 * E), F32), pltpu.VMEM((TOK, 8 * E), F32),
            dma((144,)), dma((7,)), dma((7,)), dma((7,)), dma((7,)), dma((8,)),
            dma((7,)), dma((7,)), dma((7,)), dma((7,)), dma((7,)), dma((7,)),
            dma((16,)), dma((16,)), dma((4,)), dma((6,)),
            dma((16,)), dma(()), dma((4,)), dma((3,)), dma((2,)), dma((6,)), dma((6,)), dma((4,)), dma((3,)),
            pltpu.SemaphoreType.REGULAR, pltpu.SemaphoreType.REGULAR,
        ],
        compiler_params=pltpu.CompilerParams(
            collective_id=0, has_side_effects=True, vmem_limit_bytes=48 * 1024 * 1024
        ),
        cost_estimate=pl.CostEstimate(flops=4_000_000_000, bytes_accessed=200_000_000, transcendentals=1 << 20),
    )(queries, keys, values, ids, weight)


def on_device(queries, keys, values, cluster_ids, out_weight):
    q, k, v = (jnp.transpose(a, (1, 0, 2)) for a in (queries, keys, values))
    return chain(q, k, v, cluster_ids.T, out_weight)


def solution(mesh):
    placed = (
        P("seq", "head", None),
        P("seq", "head", None),
        P("seq", "head", None),
        P("seq", "head"),
        P("seq", "head"),
    )
    return jax.shard_map(
        on_device, mesh=mesh, in_specs=placed, out_specs=P("seq", "head"), check_vma=False
    )
```

```python
import math

import jax
import jax.numpy as jnp
from jax import lax
from jax.experimental import pallas as pl
from jax.experimental.pallas import tpu as pltpu
from jax.sharding import PartitionSpec as P

C = 512
E = 128
NY, NZ, NX = 4, 8, 4
TOK = 256
BLK = C // NZ
HALF = E // 2
EXP2_SCALE = math.log2(math.e) / math.sqrt(E)
F32, BF16 = jnp.float32, jnp.bfloat16
SIDE = 384
SUM_T, OUT_T, PAIR_T = BF16, BF16, BF16


def chain_kernel(
    q_ref, k_ref, v_ref, ids_ref, w_ref, out_ref,
    qbuf, kbuf, vbuf, idst, idbuf, idxbuf, acc, msg_t, msg_c, msg_o, msg_m, recv_t, recv_c, recv_o, recv_m, cent, sbuf, mx, ls, oacc,
    att, idrow, idcol, wbuf, feat, psum, give, other,
    ssem, rq, rk, rv, rid, ridx, rt, rtc, rc, ro, rom, rz, ra, rb, rf, lsem, swc, rwo, rw1, rwr, rwl, rwy, rwa, rwra, rwla, zup, zdown,
):
    s_id, x = lax.axis_index("seq"), lax.axis_index("head")
    c = lax.rem(s_id, 2)
    z = lax.rem(lax.div(s_id, 2), NZ)
    y = lax.div(s_id, 2 * NZ)
    yc = y * 2 + c
    g0 = x * NY + y

    def seq_of(yy, zz, cc):
        return (yy * NZ + zz) * 2 + cc

    sends = []

    def put(src, dst, rsem, seq, head):
        cp = pltpu.make_async_remote_copy(
            src_ref=src, dst_ref=dst, send_sem=ssem.at[len(sends)], recv_sem=rsem,
            device_id=(seq, head), device_id_type=pl.DeviceIdType.MESH,
        )
        cp.start()
        sends.append(cp)
        return cp

    maybe = []

    def put_if(cond, src, dst, rsem, seq, head):
        cp = pltpu.make_async_remote_copy(
            src_ref=src, dst_ref=dst, send_sem=swc.at[len(maybe)], recv_sem=rsem,
            device_id=(seq, head), device_id_type=pl.DeviceIdType.MESH,
        )
        pl.when(cond)(cp.start)
        maybe.append((cond, cp))

    def arrived(ref, rsem):
        pltpu.make_async_copy(ref, ref, rsem).wait()

    def yc_peer(d):
        t = lax.rem(yc + d, 8)
        return lax.div(t, 2), lax.rem(t, 2)

    barrier = pltpu.get_barrier_semaphore()

    def greet(seq, head):
        pl.semaphore_signal(barrier, inc=1, device_id=(seq, head), device_id_type=pl.DeviceIdType.MESH)

    for d in range(1, 8):
        ty, tc = yc_peer(d)
        greet(seq_of(ty, z, tc), x)
    for step in (1, NZ - 1):
        greet(seq_of(y, lax.rem(z + step, NZ), 0), x)
        greet(seq_of(y, lax.rem(z + step, NZ), 1), x)
    for e in range(1, NX):
        greet(s_id, lax.rem(x + e, NX))
        greet(seq_of(y, z, 1 - c), lax.rem(x + e, NX))

    for h in range(8):
        idst[h] = ids_ref[pl.ds(h, 1), :]
    local = []
    own_h = c * NY + y
    for n, (src, dst) in enumerate(
        ((idst.at[own_h], idbuf.at[yc]), (q_ref.at[own_h], qbuf.at[yc]),
         (k_ref.at[own_h], kbuf.at[yc]), (v_ref.at[own_h], vbuf.at[yc]),
         (ids_ref, idxbuf.at[c]))
    ):
        cp = pltpu.make_async_copy(src, dst, lsem.at[n])
        cp.start()
        local.append(cp)

    pl.semaphore_wait(barrier, 17)

    for d in range(1, 8):
        ty, tc = yc_peer(d)
        put(idst.at[tc * NY + ty], idbuf.at[yc], rid.at[d - 1], seq_of(ty, z, tc), x)
    for d in range(1, 8):
        ty, tc = yc_peer(d)
        put(q_ref.at[tc * NY + ty], qbuf.at[yc], rq.at[d - 1], seq_of(ty, z, tc), x)
    put(ids_ref, idxbuf.at[c], ridx.at[1], seq_of(y, z, 1 - c), x)
    for e in range(1, NX):
        for f in range(2):
            tc = lax.rem(c + f, 2)
            put(ids_ref, idxbuf.at[(NX - e) * 2 + c], ridx.at[(NX - e) * 2 + f],
                seq_of(y, z, tc), lax.rem(x + e, NX))
    for src, buf, sem in ((k_ref, kbuf, rk), (v_ref, vbuf, rv)):
        for d in range(1, 8):
            ty, tc = yc_peer(d)
            put(src.at[tc * NY + ty], buf.at[yc], sem.at[d - 1], seq_of(ty, z, tc), x)

    home = lax.div(z, NZ // 2)
    half_rows = pl.ds(pl.multiple_of(c * HALF, HALF), HALF)
    other_rows = pl.ds(pl.multiple_of((1 - c) * HALF, HALF), HALF)

    def w_held(o):
        return lax.div(o, NZ // 2) == c

    left_cols, right_cols = pl.ds(0, SIDE), pl.ds(SIDE, 8 * E - SIDE)

    def w_b(o):
        return wbuf.at[y, lax.rem(o, NY), :, right_cols]

    def w_a(o):
        return wbuf.at[:, lax.rem(o, NY), :, left_cols]

    w_own = wbuf.at[y, lax.rem(z, NY), half_rows]
    w_copy = pltpu.make_async_copy(w_ref, w_own, lsem.at[5])
    pl.when(home == c)(w_copy.start)
    put_if(home != c, w_ref, w_own, rwo, seq_of(y, z, 1 - c), x)
    own_b = wbuf.at[y, lax.rem(z, NY), half_rows, right_cols]
    for step, sem in ((1, 0), (NZ - 1, 2)):
        put(w_ref.at[:, right_cols], own_b, rw1.at[sem + c], seq_of(y, lax.rem(z + step, NZ), home), x)

    def w_side():
        own_a = wbuf.at[y, lax.rem(z, NY), half_rows, left_cols]
        for e in range(1, NY):
            put(w_ref.at[:, left_cols], own_a, rwa.at[(e - 1) * 2 + c], seq_of(lax.rem(y + e, NY), z, home), x)

    w_side()

    def w_turn(k, far, sems, base):
        o = lax.rem(z + far * k, NZ)

        @pl.when(w_held(o))
        def _():
            if k == 1:
                for cc in range(2):
                    arrived(wbuf.at[y, lax.rem(o, NY), pl.ds(cc * HALF, HALF), right_cols], rw1.at[base + cc])
            else:
                arrived(w_b(o), sems.at[k - 2])

        return o

    def w_step(k):
        o = w_turn(k, NZ - 1, rwr, 0)
        put_if(w_held(o), w_b(o), w_b(o), rwr.at[k - 1], seq_of(y, lax.rem(z + 1, NZ), c), x)
        if k < 3:
            o = w_turn(k, 1, rwl, 2)
            put_if(w_held(o), w_b(o), w_b(o), rwl.at[k - 1], seq_of(y, lax.rem(z + NZ - 1, NZ), c), x)

    def w_spread():
        w_turn(4, NZ - 1, rwr, 0)
        w_turn(3, 1, rwl, 2)

        @pl.when(home == c)
        def _():
            w_copy.wait()
            arrived(wbuf.at[y, lax.rem(z, NY), other_rows], rwo)

        up, down = seq_of(lax.rem(y + 1, NY), z, c), seq_of(lax.rem(y + NY - 1, NY), z, c)
        for n, (lo, to) in enumerate(((0, up), (2, down), (2, up), (0, down))):
            rows = wbuf.at[y, pl.ds(lo, 2), :, right_cols]
            put(rows, rows, rwy.at[n], to, x)

    def w_relay():
        below, above = lax.rem(y + NY - 1, NY), lax.rem(y + 1, NY)
        first = wbuf.at[below, pl.ds(0, 2), :, right_cols]
        arrived(first, rwy.at[0])
        put(first, first, rwy.at[4], seq_of(above, z, c), x)
        second = wbuf.at[above, pl.ds(2, 2), :, right_cols]
        arrived(second, rwy.at[1])
        put(second, second, rwy.at[5], seq_of(below, z, c), x)

    def w_finish():
        below, above, across = lax.rem(y + NY - 1, NY), lax.rem(y + 1, NY), lax.rem(y + 2, NY)
        arrived(wbuf.at[below, pl.ds(2, 2), :, right_cols], rwy.at[2])
        arrived(wbuf.at[above, pl.ds(0, 2), :, right_cols], rwy.at[3])
        arrived(wbuf.at[across, pl.ds(0, 2), :, right_cols], rwy.at[4])
        arrived(wbuf.at[across, pl.ds(2, 2), :, right_cols], rwy.at[5])
        a_wait(4, NZ - 1, rwra)
        a_wait(3, 1, rwla)

    def a_wait(k, far, sems):
        o = lax.rem(z + far * k, NZ)

        @pl.when(w_held(o))
        def _():
            arrived(w_a(o), sems.at[k - 1])

    def a_step(k):
        if k == 0:
            @pl.when(home == c)
            def _():
                for e in range(1, NY):
                    for cc in range(2):
                        arrived(wbuf.at[lax.rem(y + NY - e, NY), lax.rem(z, NY), pl.ds(cc * HALF, HALF), left_cols],
                                rwa.at[(e - 1) * 2 + cc])
        else:
            a_wait(k, NZ - 1, rwra)
            if k < 3:
                a_wait(k, 1, rwla)
        o = lax.rem(z + (NZ - 1) * k, NZ)
        put_if(w_held(o), w_a(o), w_a(o), rwra.at[k], seq_of(y, lax.rem(z + 1, NZ), c), x)
        if k < 3:
            o = lax.rem(z + k, NZ)
            put_if(w_held(o), w_a(o), w_a(o), rwla.at[k], seq_of(y, lax.rem(z + NZ - 1, NZ), c), x)

    def take8(buf, sem):
        for d in range(1, 8):
            arrived(buf.at[lax.rem(yc + 8 - d, 8)], sem.at[d - 1])

    eye = lax.broadcasted_iota(jnp.int32, (BLK, E), 0) == lax.broadcasted_iota(jnp.int32, (BLK, E), 1)

    def to_row(col):
        return jnp.sum(jnp.where(eye, col, 0.0), axis=0, keepdims=True)

    def to_col(row):
        return jnp.sum(jnp.where(eye, row, 0.0), axis=1, keepdims=True)

    local[0].wait()
    local[1].wait()
    acc[...] = jnp.zeros_like(acc)
    for k in range(3):
        pl.semaphore_signal(zup, inc=1, device_id=(seq_of(y, lax.rem(z + 1, NZ), c), x), device_id_type=pl.DeviceIdType.MESH)
        if k < 2:
            pl.semaphore_signal(zdown, inc=1, device_id=(seq_of(y, lax.rem(z + NZ - 1, NZ), c), x), device_id_type=pl.DeviceIdType.MESH)
            pl.semaphore_wait(zdown, 1)
        pl.semaphore_wait(zup, 1)
    w_step(1)
    w_step(2)

    @pl.loop(0, 8)
    def _(d):
        i = lax.rem(yc + 8 - d, 8)

        @pl.when(d > 0)
        def _():
            arrived(idbuf.at[i], rid.at[d - 1])
            arrived(qbuf.at[i], rq.at[d - 1])

        label = lax.broadcasted_iota(jnp.int32, (C, TOK), 0)
        onehot = (label == idbuf[i]).astype(F32).astype(BF16)
        rhs = jnp.concatenate([qbuf[i], jnp.ones((TOK, E), BF16)], axis=1)
        acc[...] += jnp.dot(onehot, rhs, preferred_element_type=F32)

    @pl.loop(0, NZ)
    def _(b):
        rows = pl.ds(pl.multiple_of(b * BLK, BLK), BLK)
        msg_t[b] = acc[rows, pl.ds(0, E)].astype(SUM_T)
        msg_c[b] = jnp.broadcast_to(to_row(acc[rows, pl.ds(E, E)]), (8, E))

    for d in (4, 3, 5, 2, 6, 1, 7):
        tz = lax.rem(z + d, NZ)
        put(msg_c.at[tz], recv_c.at[d - 1], rtc.at[d - 1], seq_of(y, tz, c), x)
        put(msg_t.at[tz], recv_t.at[d - 1], rt.at[d - 1], seq_of(y, tz, c), x)

    w_step(3)
    local[4].wait()
    for j in range(1, 8):
        e, f = j // 2, j % 2
        arrived(idxbuf.at[e * 2 + lax.rem(c + f, 2)], ridx.at[j])
    idrow[...] = jnp.zeros_like(idrow)
    for e in range(NX):
        for dy in range(NY):
            for part in range(2):
                row = idxbuf[e * 2 + part, pl.ds(c * NY + lax.rem(y + dy, NY), 1), :]
                idrow[pl.ds(e * 8 + dy, 1), pl.ds(part * TOK, TOK)] = row.astype(F32)
    idcol[...] = idrow[...].T

    total, count = msg_t[z].astype(F32), msg_c[z]
    for d in range(1, NZ):
        arrived(recv_c.at[d - 1], rtc.at[d - 1])
        arrived(recv_t.at[d - 1], rt.at[d - 1])
        total = total + recv_t[d - 1].astype(F32)
        count = count + recv_c[d - 1]
    count = to_col(count[:1])
    cent[z] = (total / jnp.maximum(count, 1.0)).astype(BF16)

    for d in (4, 3, 5, 2, 6, 1, 7):
        tz = lax.rem(z + d, NZ)
        put(cent.at[z], cent.at[z], rc.at[d - 1], seq_of(y, tz, c), x)
    w_spread()
    local[2].wait()
    take8(kbuf, rk)
    for d in range(1, NZ):
        arrived(cent.at[lax.rem(z + NZ - d, NZ)], rc.at[d - 1])

    a_step(0)
    half = C // 2
    for part, dist in enumerate(((4, 3, 5, 2), (6, 1, 7, 0))):
        centroid = jnp.concatenate([cent[lax.rem(z + d, NZ)] for d in dist], axis=0)
        mx[...] = jnp.full_like(mx, -jnp.inf)

        @pl.loop(0, 8)
        def _(i):
            s = lax.dot_general(centroid, kbuf[i], (((1,), (1,)), ((), ())), preferred_element_type=F32)
            sbuf[i] = s
            mx[...] = jnp.maximum(mx[...], jnp.maximum(s[:, :E], s[:, E:]))

        mx[...] = jnp.broadcast_to(jnp.max(mx[...], axis=1, keepdims=True), (half, E))
        ls[...] = jnp.zeros_like(ls)
        if part == 0:
            local[3].wait()
            take8(vbuf, rv)
        oacc[...] = jnp.zeros_like(oacc)

        @pl.loop(0, 8)
        def _(i):
            m = mx[...]
            p = jnp.exp2((sbuf[i] - jnp.concatenate([m, m], axis=1)) * EXP2_SCALE)
            ls[...] += p[:, :E] + p[:, E:]
            oacc[...] += jnp.dot(p.astype(BF16), vbuf[i], preferred_element_type=F32)

        ls[...] = jnp.broadcast_to(jnp.sum(ls[...], axis=1, keepdims=True), (half, E))
        first = lax.broadcasted_iota(jnp.int32, (8, E), 0) == 0
        for j, d in enumerate(dist):
            rows = pl.ds(j * BLK, BLK)
            msg_m[d] = jnp.where(first, to_row(mx[rows, :]), to_row(ls[rows, :]))
            msg_o[d] = oacc[rows, :].astype(OUT_T)
            if d > 0:
                tz = lax.rem(z + d, NZ)
                put(msg_m.at[d], recv_m.at[d - 1], rom.at[d - 1], seq_of(y, tz, c), x)
                put(msg_o.at[d], recv_o.at[d - 1], ro.at[d - 1], seq_of(y, tz, c), x)

    w_relay()
    a_step(1)
    stats, parts = [msg_m[0]], [msg_o[0]]
    for d in range(1, NZ):
        arrived(recv_m.at[d - 1], rom.at[d - 1])
        arrived(recv_o.at[d - 1], ro.at[d - 1])
        stats.append(recv_m[d - 1])
        parts.append(recv_o[d - 1])
    tops = [to_col(stat[:1]) for stat in stats]
    largest = tops[0]
    for t in tops[1:]:
        largest = jnp.maximum(largest, t)
    num, den = 0.0, 0.0
    for stat, part, t in zip(stats, parts, tops):
        factor = jnp.exp2((t - largest) * EXP2_SCALE)
        num = num + part.astype(F32) * factor
        den = den + to_col(stat[1:2]) * factor
    att[g0, z] = (num / den).astype(BF16)

    for d in (4, 3, 5, 2, 6, 1, 7):
        tz = lax.rem(z + d, NZ)
        put(att.at[g0, z], att.at[g0, z], rz.at[d - 1], seq_of(y, tz, c), x)
    a_step(2)
    for d in range(1, NZ):
        arrived(att.at[g0, lax.rem(z + NZ - d, NZ)], rz.at[d - 1])

    low, high = pl.ds(0, NZ // 2), pl.ds(NZ // 2, NZ // 2)

    def g_of(dx, dy):
        return lax.rem(x + dx, NX) * NY + lax.rem(y + dy, NY)

    def to_y(g, part, sem, dx):
        for e in range(1, NY):
            put(att.at[g, part], att.at[g, part], sem.at[dx * NY + NY - e],
                seq_of(lax.rem(y + e, NY), z, c), x)

    def to_x(g, part, sem, dy):
        for e in range(1, NX):
            put(att.at[g, part], att.at[g, part], sem.at[(NX - e) * NY + dy],
                s_id, lax.rem(x + e, NX))

    to_y(g0, low, ra, 0)
    to_x(g0, high, rb, 0)
    to_x(g0, low, ra, 0)
    to_y(g0, high, rb, 0)
    a_step(3)
    for e in range(1, NY):
        arrived(att.at[g_of(0, e), low], ra.at[e])
        to_x(g_of(0, e), low, ra, e)
        arrived(att.at[g_of(e, 0), high], rb.at[e * NY])
        to_y(g_of(e, 0), high, rb, e)

    lanes = lax.broadcasted_iota(jnp.int32, (2 * TOK, C), 1).astype(F32)
    groups = (
        ((0, 0), (0, 1), (0, 2), (0, 3), (1, 0), (2, 0), (3, 0)),
        ((1, 1), (1, 2), (2, 1), (2, 2)),
        ((1, 3), (3, 1), (2, 3), (3, 2), (3, 3)),
    )
    mine = pl.ds(pl.multiple_of(c * TOK, TOK), TOK)
    theirs = pl.ds(pl.multiple_of((1 - c) * TOK, TOK), TOK)
    for at, heads in enumerate(groups):
        for n, (dx, dy) in enumerate(heads):
            g = g_of(dx, dy)
            if dx > 0:
                arrived(att.at[g, low], ra.at[dx * NY + dy])
            if dy > 0:
                arrived(att.at[g, high], rb.at[dx * NY + dy])
            col = idcol[:, pl.ds(dx * 8 + dy, 1)]
            onehot = (lanes == col).astype(F32).astype(BF16)
            picked = jnp.dot(onehot, att[g].reshape(C, E), preferred_element_type=F32)
            feat[:, pl.ds(n * E, E)] = picked.astype(BF16)
        if at == 0:
            w_finish()

        def term(rows, cols):
            block = jnp.concatenate(
                [wbuf[lax.rem(x + dx, NX), lax.rem(y + dy, NY), :, cols] for dx, dy in heads], axis=0
            )
            return jnp.dot(feat[rows, pl.ds(0, len(heads) * E)], block, preferred_element_type=F32)

        if at < len(groups) - 1:
            @pl.loop(0, NX)
            def _(n):
                cols = pl.ds(pl.multiple_of(n * TOK, TOK), TOK)
                if at == 0:
                    psum[:, cols] = term(slice(None), cols)
                else:
                    psum[:, cols] += term(slice(None), cols)
        else:
            for n in range(NX):
                cols = pl.ds(n * TOK, TOK)
                give[:, cols] = (psum[theirs, cols] + term(theirs, cols)).astype(PAIR_T)
                put(give.at[:, cols], other.at[:, cols], rf.at[n], seq_of(y, z, 1 - c), x)
            for n in range(NX):
                cols = pl.ds(n * TOK, TOK)
                total = psum[mine, cols] + term(mine, cols)
                arrived(other.at[:, cols], rf.at[n])
                out_ref[:, cols] = (total + other[:, cols].astype(F32)).astype(BF16)
    for cp in sends:
        cp.wait_send()
    for cond, cp in maybe:
        pl.when(cond)(cp.wait_send)


def chain(queries, keys, values, ids, weight):
    vmem = pl.BlockSpec(memory_space=pltpu.VMEM)
    anyw = pl.BlockSpec(memory_space=pl.ANY)
    dma = pltpu.SemaphoreType.DMA
    return pl.pallas_call(
        chain_kernel,
        out_shape=jax.ShapeDtypeStruct((TOK, 8 * E), BF16),
        in_specs=[anyw, anyw, anyw, vmem, anyw],
        out_specs=vmem,
        scratch_shapes=[
            pltpu.VMEM((8, TOK, E), BF16), pltpu.VMEM((8, TOK, E), BF16), pltpu.VMEM((8, TOK, E), BF16),
            pltpu.VMEM((8, 1, TOK), jnp.int32), pltpu.VMEM((8, 1, TOK), jnp.int32), pltpu.VMEM((8, 8, TOK), jnp.int32),
            pltpu.VMEM((C, 2 * E), F32),
            pltpu.VMEM((NZ, BLK, E), SUM_T), pltpu.VMEM((NZ, 8, E), F32),
            pltpu.VMEM((NZ, BLK, E), OUT_T), pltpu.VMEM((NZ, 8, E), F32),
            pltpu.VMEM((NZ - 1, BLK, E), SUM_T), pltpu.VMEM((NZ - 1, 8, E), F32),
            pltpu.VMEM((NZ - 1, BLK, E), OUT_T), pltpu.VMEM((NZ - 1, 8, E), F32),
            pltpu.VMEM((NZ, BLK, E), BF16), pltpu.VMEM((8, C // 2, TOK), F32),
            pltpu.VMEM((C // 2, E), F32), pltpu.VMEM((C // 2, E), F32), pltpu.VMEM((C // 2, E), F32),
            pltpu.VMEM((16, NZ, BLK, E), BF16), pltpu.VMEM((E, 2 * TOK), F32), pltpu.VMEM((2 * TOK, E), F32),
            pltpu.VMEM((NX, NY, E, 8 * E), BF16), pltpu.VMEM((2 * TOK, 16 * E), BF16),
            pltpu.VMEM((2 * TOK, 8 * E), F32), pltpu.VMEM((TOK, 8 * E), PAIR_T),
            pltpu.VMEM((TOK, 8 * E), PAIR_T),
            dma((144,)), dma((7,)), dma((7,)), dma((7,)), dma((7,)), dma((8,)),
            dma((7,)), dma((7,)), dma((7,)), dma((7,)), dma((7,)), dma((7,)),
            dma((16,)), dma((16,)), dma((4,)), dma((6,)),
            dma((16,)), dma(()), dma((4,)), dma((3,)), dma((2,)), dma((6,)), dma((6,)), dma((4,)), dma((3,)),
            pltpu.SemaphoreType.REGULAR, pltpu.SemaphoreType.REGULAR,
        ],
        compiler_params=pltpu.CompilerParams(
            collective_id=0, has_side_effects=True, vmem_limit_bytes=48 * 1024 * 1024
        ),
        cost_estimate=pl.CostEstimate(flops=4_000_000_000, bytes_accessed=200_000_000, transcendentals=1 << 20),
    )(queries, keys, values, ids, weight)


def on_device(queries, keys, values, cluster_ids, out_weight):
    q, k, v = (jnp.transpose(a, (1, 0, 2)) for a in (queries, keys, values))
    return chain(q, k, v, cluster_ids.T, out_weight)


def solution(mesh):
    placed = (
        P("seq", "head", None),
        P("seq", "head", None),
        P("seq", "head", None),
        P("seq", "head"),
        P("seq", "head"),
    )
    return jax.shard_map(
        on_device, mesh=mesh, in_specs=placed, out_specs=P("seq", "head"), check_vma=False
    )
```

```python
import math

import jax
import jax.numpy as jnp
from jax import lax
from jax.experimental import pallas as pl
from jax.experimental.pallas import tpu as pltpu
from jax.sharding import PartitionSpec as P

C = 512
E = 128
NY, NZ, NX = 4, 8, 4
TOK = 256
BLK = C // NZ
HALF = E // 2
EXP2_SCALE = math.log2(math.e) / math.sqrt(E)
F32, BF16 = jnp.float32, jnp.bfloat16
SIDE = 384
SUM_T, OUT_T, PAIR_T = BF16, BF16, BF16


def chain_kernel(
    q_ref, k_ref, v_ref, ids_ref, w_ref, out_ref,
    qbuf, kbuf, vbuf, idst, idbuf, idxbuf, acc, msg_t, msg_c, msg_o, msg_m, recv_t, recv_c, recv_o, recv_m, cent, sbuf, mx, ls, oacc,
    att, idrow, idcol, wbuf, feat, psum, give, other,
    ssem, rq, rk, rv, rid, ridx, rt, rtc, rc, ro, rom, rz, ra, rb, rf, lsem, swc, rwo, rw1, rwr, rwl, rwy, rwa, rwra, rwla, zup, zdown,
):
    s_id, x = lax.axis_index("seq"), lax.axis_index("head")
    c = lax.rem(s_id, 2)
    z = lax.rem(lax.div(s_id, 2), NZ)
    y = lax.div(s_id, 2 * NZ)
    yc = y * 2 + c
    g0 = x * NY + y

    def seq_of(yy, zz, cc):
        return (yy * NZ + zz) * 2 + cc

    sends = []

    def put(src, dst, rsem, seq, head):
        cp = pltpu.make_async_remote_copy(
            src_ref=src, dst_ref=dst, send_sem=ssem.at[len(sends)], recv_sem=rsem,
            device_id=(seq, head), device_id_type=pl.DeviceIdType.MESH,
        )
        cp.start()
        sends.append(cp)
        return cp

    maybe = []

    def put_if(cond, src, dst, rsem, seq, head):
        cp = pltpu.make_async_remote_copy(
            src_ref=src, dst_ref=dst, send_sem=swc.at[len(maybe)], recv_sem=rsem,
            device_id=(seq, head), device_id_type=pl.DeviceIdType.MESH,
        )
        pl.when(cond)(cp.start)
        maybe.append((cond, cp))

    def arrived(ref, rsem):
        pltpu.make_async_copy(ref, ref, rsem).wait()

    def yc_peer(d):
        t = lax.rem(yc + d, 8)
        return lax.div(t, 2), lax.rem(t, 2)

    barrier = pltpu.get_barrier_semaphore()

    def greet(seq, head):
        pl.semaphore_signal(barrier, inc=1, device_id=(seq, head), device_id_type=pl.DeviceIdType.MESH)

    for d in range(1, 8):
        ty, tc = yc_peer(d)
        greet(seq_of(ty, z, tc), x)
    for step in (1, NZ - 1):
        greet(seq_of(y, lax.rem(z + step, NZ), 0), x)
        greet(seq_of(y, lax.rem(z + step, NZ), 1), x)
    for e in range(1, NX):
        greet(s_id, lax.rem(x + e, NX))
        greet(seq_of(y, z, 1 - c), lax.rem(x + e, NX))

    for h in range(8):
        idst[h] = ids_ref[pl.ds(h, 1), :]
    local = []
    own_h = c * NY + y
    for n, (src, dst) in enumerate(
        ((idst.at[own_h], idbuf.at[yc]), (q_ref.at[own_h], qbuf.at[yc]),
         (k_ref.at[own_h], kbuf.at[yc]), (v_ref.at[own_h], vbuf.at[yc]),
         (ids_ref, idxbuf.at[c]))
    ):
        cp = pltpu.make_async_copy(src, dst, lsem.at[n])
        cp.start()
        local.append(cp)

    pl.semaphore_wait(barrier, 17)

    for d in range(1, 8):
        ty, tc = yc_peer(d)
        put(idst.at[tc * NY + ty], idbuf.at[yc], rid.at[d - 1], seq_of(ty, z, tc), x)
    for d in range(1, 8):
        ty, tc = yc_peer(d)
        put(q_ref.at[tc * NY + ty], qbuf.at[yc], rq.at[d - 1], seq_of(ty, z, tc), x)
    put(ids_ref, idxbuf.at[c], ridx.at[1], seq_of(y, z, 1 - c), x)
    for e in range(1, NX):
        for f in range(2):
            tc = lax.rem(c + f, 2)
            put(ids_ref, idxbuf.at[(NX - e) * 2 + c], ridx.at[(NX - e) * 2 + f],
                seq_of(y, z, tc), lax.rem(x + e, NX))
    for src, buf, sem in ((k_ref, kbuf, rk), (v_ref, vbuf, rv)):
        for d in range(1, 8):
            ty, tc = yc_peer(d)
            put(src.at[tc * NY + ty], buf.at[yc], sem.at[d - 1], seq_of(ty, z, tc), x)

    home = lax.div(z, NZ // 2)
    half_rows = pl.ds(pl.multiple_of(c * HALF, HALF), HALF)
    other_rows = pl.ds(pl.multiple_of((1 - c) * HALF, HALF), HALF)

    def w_held(o):
        return lax.div(o, NZ // 2) == c

    left_cols, right_cols = pl.ds(0, SIDE), pl.ds(SIDE, 8 * E - SIDE)

    def w_b(o):
        return wbuf.at[y, lax.rem(o, NY), :, right_cols]

    def w_a(o):
        return wbuf.at[:, lax.rem(o, NY), :, left_cols]

    w_own = wbuf.at[y, lax.rem(z, NY), half_rows]
    w_copy = pltpu.make_async_copy(w_ref, w_own, lsem.at[5])
    pl.when(home == c)(w_copy.start)
    put_if(home != c, w_ref, w_own, rwo, seq_of(y, z, 1 - c), x)
    own_b = wbuf.at[y, lax.rem(z, NY), half_rows, right_cols]
    for step, sem in ((1, 0), (NZ - 1, 2)):
        put(w_ref.at[:, right_cols], own_b, rw1.at[sem + c], seq_of(y, lax.rem(z + step, NZ), home), x)

    def w_side():
        own_a = wbuf.at[y, lax.rem(z, NY), half_rows, left_cols]
        for e in range(1, NY):
            put(w_ref.at[:, left_cols], own_a, rwa.at[(e - 1) * 2 + c], seq_of(lax.rem(y + e, NY), z, home), x)

    w_side()

    def w_turn(k, far, sems, base):
        o = lax.rem(z + far * k, NZ)

        @pl.when(w_held(o))
        def _():
            if k == 1:
                for cc in range(2):
                    arrived(wbuf.at[y, lax.rem(o, NY), pl.ds(cc * HALF, HALF), right_cols], rw1.at[base + cc])
            else:
                arrived(w_b(o), sems.at[k - 2])

        return o

    def w_step(k):
        o = w_turn(k, NZ - 1, rwr, 0)
        put_if(w_held(o), w_b(o), w_b(o), rwr.at[k - 1], seq_of(y, lax.rem(z + 1, NZ), c), x)
        if k < 3:
            o = w_turn(k, 1, rwl, 2)
            put_if(w_held(o), w_b(o), w_b(o), rwl.at[k - 1], seq_of(y, lax.rem(z + NZ - 1, NZ), c), x)

    def w_spread():
        w_turn(4, NZ - 1, rwr, 0)
        w_turn(3, 1, rwl, 2)

        @pl.when(home == c)
        def _():
            w_copy.wait()
            arrived(wbuf.at[y, lax.rem(z, NY), other_rows], rwo)

        up, down = seq_of(lax.rem(y + 1, NY), z, c), seq_of(lax.rem(y + NY - 1, NY), z, c)
        for n, (lo, to) in enumerate(((0, up), (2, down), (2, up), (0, down))):
            rows = wbuf.at[y, pl.ds(lo, 2), :, right_cols]
            put(rows, rows, rwy.at[n], to, x)

    def w_relay():
        below, above = lax.rem(y + NY - 1, NY), lax.rem(y + 1, NY)
        first = wbuf.at[below, pl.ds(0, 2), :, right_cols]
        arrived(first, rwy.at[0])
        put(first, first, rwy.at[4], seq_of(above, z, c), x)
        second = wbuf.at[above, pl.ds(2, 2), :, right_cols]
        arrived(second, rwy.at[1])
        put(second, second, rwy.at[5], seq_of(below, z, c), x)

    def w_finish():
        below, above, across = lax.rem(y + NY - 1, NY), lax.rem(y + 1, NY), lax.rem(y + 2, NY)
        arrived(wbuf.at[below, pl.ds(2, 2), :, right_cols], rwy.at[2])
        arrived(wbuf.at[above, pl.ds(0, 2), :, right_cols], rwy.at[3])
        arrived(wbuf.at[across, pl.ds(0, 2), :, right_cols], rwy.at[4])
        arrived(wbuf.at[across, pl.ds(2, 2), :, right_cols], rwy.at[5])
        a_wait(4, NZ - 1, rwra)
        a_wait(3, 1, rwla)

    def a_wait(k, far, sems):
        o = lax.rem(z + far * k, NZ)

        @pl.when(w_held(o))
        def _():
            arrived(w_a(o), sems.at[k - 1])

    def a_step(k):
        if k == 0:
            @pl.when(home == c)
            def _():
                for e in range(1, NY):
                    for cc in range(2):
                        arrived(wbuf.at[lax.rem(y + NY - e, NY), lax.rem(z, NY), pl.ds(cc * HALF, HALF), left_cols],
                                rwa.at[(e - 1) * 2 + cc])
        else:
            a_wait(k, NZ - 1, rwra)
            if k < 3:
                a_wait(k, 1, rwla)
        o = lax.rem(z + (NZ - 1) * k, NZ)
        put_if(w_held(o), w_a(o), w_a(o), rwra.at[k], seq_of(y, lax.rem(z + 1, NZ), c), x)
        if k < 3:
            o = lax.rem(z + k, NZ)
            put_if(w_held(o), w_a(o), w_a(o), rwla.at[k], seq_of(y, lax.rem(z + NZ - 1, NZ), c), x)

    def take8(buf, sem):
        for d in range(1, 8):
            arrived(buf.at[lax.rem(yc + 8 - d, 8)], sem.at[d - 1])

    eye = lax.broadcasted_iota(jnp.int32, (BLK, E), 0) == lax.broadcasted_iota(jnp.int32, (BLK, E), 1)

    def to_row(col):
        return jnp.sum(jnp.where(eye, col, 0.0), axis=0, keepdims=True)

    def to_col(row):
        return jnp.sum(jnp.where(eye, row, 0.0), axis=1, keepdims=True)

    local[0].wait()
    local[1].wait()
    acc[...] = jnp.zeros_like(acc)
    for k in range(3):
        pl.semaphore_signal(zup, inc=1, device_id=(seq_of(y, lax.rem(z + 1, NZ), c), x), device_id_type=pl.DeviceIdType.MESH)
        if k < 2:
            pl.semaphore_signal(zdown, inc=1, device_id=(seq_of(y, lax.rem(z + NZ - 1, NZ), c), x), device_id_type=pl.DeviceIdType.MESH)
            pl.semaphore_wait(zdown, 1)
        pl.semaphore_wait(zup, 1)
    w_step(1)
    w_step(2)

    @pl.loop(0, 8)
    def _(d):
        i = lax.rem(yc + 8 - d, 8)

        @pl.when(d > 0)
        def _():
            arrived(idbuf.at[i], rid.at[d - 1])
            arrived(qbuf.at[i], rq.at[d - 1])

        label = lax.broadcasted_iota(jnp.int32, (C, TOK), 0)
        onehot = (label == idbuf[i]).astype(F32).astype(BF16)
        rhs = jnp.concatenate([qbuf[i], jnp.ones((TOK, E), BF16)], axis=1)
        acc[...] += jnp.dot(onehot, rhs, preferred_element_type=F32)

    @pl.loop(0, NZ)
    def _(b):
        rows = pl.ds(pl.multiple_of(b * BLK, BLK), BLK)
        msg_t[b] = acc[rows, pl.ds(0, E)].astype(SUM_T)
        msg_c[b] = jnp.broadcast_to(to_row(acc[rows, pl.ds(E, E)]), (8, E))

    for d in (4, 3, 5, 2, 6, 1, 7):
        tz = lax.rem(z + d, NZ)
        put(msg_c.at[tz], recv_c.at[d - 1], rtc.at[d - 1], seq_of(y, tz, c), x)
        put(msg_t.at[tz], recv_t.at[d - 1], rt.at[d - 1], seq_of(y, tz, c), x)

    w_step(3)
    local[4].wait()
    for j in range(1, 8):
        e, f = j // 2, j % 2
        arrived(idxbuf.at[e * 2 + lax.rem(c + f, 2)], ridx.at[j])
    idrow[...] = jnp.zeros_like(idrow)
    for e in range(NX):
        for dy in range(NY):
            for part in range(2):
                row = idxbuf[e * 2 + part, pl.ds(c * NY + lax.rem(y + dy, NY), 1), :]
                idrow[pl.ds(e * 8 + dy, 1), pl.ds(part * TOK, TOK)] = row.astype(F32)
    idcol[...] = idrow[...].T

    total, count = msg_t[z].astype(F32), msg_c[z]
    for d in range(1, NZ):
        arrived(recv_c.at[d - 1], rtc.at[d - 1])
        arrived(recv_t.at[d - 1], rt.at[d - 1])
        total = total + recv_t[d - 1].astype(F32)
        count = count + recv_c[d - 1]
    count = to_col(count[:1])
    cent[z] = (total / jnp.maximum(count, 1.0)).astype(BF16)

    for d in (4, 3, 5, 2, 6, 1, 7):
        tz = lax.rem(z + d, NZ)
        put(cent.at[z], cent.at[z], rc.at[d - 1], seq_of(y, tz, c), x)
    w_spread()
    local[2].wait()
    take8(kbuf, rk)
    for d in range(1, NZ):
        arrived(cent.at[lax.rem(z + NZ - d, NZ)], rc.at[d - 1])

    a_step(0)
    half = C // 2
    for part, dist in enumerate(((4, 3, 5, 2), (6, 1, 7, 0))):
        centroid = jnp.concatenate([cent[lax.rem(z + d, NZ)] for d in dist], axis=0)
        mx[...] = jnp.full_like(mx, -jnp.inf)

        @pl.loop(0, 8)
        def _(i):
            s = lax.dot_general(centroid, kbuf[i], (((1,), (1,)), ((), ())), preferred_element_type=F32)
            sbuf[i] = s
            mx[...] = jnp.maximum(mx[...], jnp.maximum(s[:, :E], s[:, E:]))

        mx[...] = jnp.broadcast_to(jnp.max(mx[...], axis=1, keepdims=True), (half, E))
        ls[...] = jnp.zeros_like(ls)
        if part == 0:
            local[3].wait()
            take8(vbuf, rv)
        oacc[...] = jnp.zeros_like(oacc)

        @pl.loop(0, 8)
        def _(i):
            m = mx[...]
            p = jnp.exp2((sbuf[i] - jnp.concatenate([m, m], axis=1)) * EXP2_SCALE)
            ls[...] += p[:, :E] + p[:, E:]
            oacc[...] += jnp.dot(p.astype(BF16), vbuf[i], preferred_element_type=F32)

        ls[...] = jnp.broadcast_to(jnp.sum(ls[...], axis=1, keepdims=True), (half, E))
        first = lax.broadcasted_iota(jnp.int32, (8, E), 0) == 0
        for j, d in enumerate(dist):
            rows = pl.ds(j * BLK, BLK)
            msg_m[d] = jnp.where(first, to_row(mx[rows, :]), to_row(ls[rows, :]))
            msg_o[d] = oacc[rows, :].astype(OUT_T)
            if d > 0:
                tz = lax.rem(z + d, NZ)
                put(msg_m.at[d], recv_m.at[d - 1], rom.at[d - 1], seq_of(y, tz, c), x)
                put(msg_o.at[d], recv_o.at[d - 1], ro.at[d - 1], seq_of(y, tz, c), x)

    w_relay()
    a_step(1)
    stats, parts = [msg_m[0]], [msg_o[0]]
    for d in range(1, NZ):
        arrived(recv_m.at[d - 1], rom.at[d - 1])
        arrived(recv_o.at[d - 1], ro.at[d - 1])
        stats.append(recv_m[d - 1])
        parts.append(recv_o[d - 1])
    tops = [to_col(stat[:1]) for stat in stats]
    largest = tops[0]
    for t in tops[1:]:
        largest = jnp.maximum(largest, t)
    num, den = 0.0, 0.0
    for stat, part, t in zip(stats, parts, tops):
        factor = jnp.exp2((t - largest) * EXP2_SCALE)
        num = num + part.astype(F32) * factor
        den = den + to_col(stat[1:2]) * factor
    att[g0, z] = (num / den).astype(BF16)

    for d in (4, 3, 5, 2, 6, 1, 7):
        tz = lax.rem(z + d, NZ)
        put(att.at[g0, z], att.at[g0, z], rz.at[d - 1], seq_of(y, tz, c), x)
    a_step(2)
    for d in range(1, NZ):
        arrived(att.at[g0, lax.rem(z + NZ - d, NZ)], rz.at[d - 1])

    low, high = pl.ds(0, NZ // 2), pl.ds(NZ // 2, NZ // 2)

    def g_of(dx, dy):
        return lax.rem(x + dx, NX) * NY + lax.rem(y + dy, NY)

    def to_y(g, part, sem, dx):
        for e in (2, 1, 3):
            put(att.at[g, part], att.at[g, part], sem.at[dx * NY + NY - e],
                seq_of(lax.rem(y + e, NY), z, c), x)

    def to_x(g, part, sem, dy):
        for e in (2, 1, 3):
            put(att.at[g, part], att.at[g, part], sem.at[(NX - e) * NY + dy],
                s_id, lax.rem(x + e, NX))

    to_y(g0, low, ra, 0)
    to_x(g0, high, rb, 0)
    to_x(g0, low, ra, 0)
    to_y(g0, high, rb, 0)
    a_step(3)
    for e in range(1, NY):
        arrived(att.at[g_of(0, e), low], ra.at[e])
        to_x(g_of(0, e), low, ra, e)
        arrived(att.at[g_of(e, 0), high], rb.at[e * NY])
        to_y(g_of(e, 0), high, rb, e)

    lanes = lax.broadcasted_iota(jnp.int32, (2 * TOK, C), 1).astype(F32)
    groups = (
        ((0, 0), (0, 1), (0, 2), (0, 3), (1, 0), (2, 0), (3, 0)),
        ((1, 1), (1, 2), (2, 1), (2, 2)),
        ((1, 3), (3, 1), (2, 3), (3, 2), (3, 3)),
    )
    mine = pl.ds(pl.multiple_of(c * TOK, TOK), TOK)
    theirs = pl.ds(pl.multiple_of((1 - c) * TOK, TOK), TOK)
    for at, heads in enumerate(groups):
        for n, (dx, dy) in enumerate(heads):
            g = g_of(dx, dy)
            if dx > 0:
                arrived(att.at[g, low], ra.at[dx * NY + dy])
            if dy > 0:
                arrived(att.at[g, high], rb.at[dx * NY + dy])
            col = idcol[:, pl.ds(dx * 8 + dy, 1)]
            onehot = (lanes == col).astype(F32).astype(BF16)
            picked = jnp.dot(onehot, att[g].reshape(C, E), preferred_element_type=F32)
            feat[:, pl.ds(n * E, E)] = picked.astype(BF16)
        if at == 0:
            w_finish()

        def term(rows, cols):
            block = jnp.concatenate(
                [wbuf[lax.rem(x + dx, NX), lax.rem(y + dy, NY), :, cols] for dx, dy in heads], axis=0
            )
            return jnp.dot(feat[rows, pl.ds(0, len(heads) * E)], block, preferred_element_type=F32)

        if at < len(groups) - 1:
            @pl.loop(0, NX)
            def _(n):
                cols = pl.ds(pl.multiple_of(n * TOK, TOK), TOK)
                if at == 0:
                    psum[:, cols] = term(slice(None), cols)
                else:
                    psum[:, cols] += term(slice(None), cols)
        else:
            for n in range(NX):
                cols = pl.ds(n * TOK, TOK)
                give[:, cols] = (psum[theirs, cols] + term(theirs, cols)).astype(PAIR_T)
                put(give.at[:, cols], other.at[:, cols], rf.at[n], seq_of(y, z, 1 - c), x)
            for n in range(NX):
                cols = pl.ds(n * TOK, TOK)
                total = psum[mine, cols] + term(mine, cols)
                arrived(other.at[:, cols], rf.at[n])
                out_ref[:, cols] = (total + other[:, cols].astype(F32)).astype(BF16)
    for cp in sends:
        cp.wait_send()
    for cond, cp in maybe:
        pl.when(cond)(cp.wait_send)


def chain(queries, keys, values, ids, weight):
    vmem = pl.BlockSpec(memory_space=pltpu.VMEM)
    anyw = pl.BlockSpec(memory_space=pl.ANY)
    dma = pltpu.SemaphoreType.DMA
    return pl.pallas_call(
        chain_kernel,
        out_shape=jax.ShapeDtypeStruct((TOK, 8 * E), BF16),
        in_specs=[anyw, anyw, anyw, vmem, anyw],
        out_specs=vmem,
        scratch_shapes=[
            pltpu.VMEM((8, TOK, E), BF16), pltpu.VMEM((8, TOK, E), BF16), pltpu.VMEM((8, TOK, E), BF16),
            pltpu.VMEM((8, 1, TOK), jnp.int32), pltpu.VMEM((8, 1, TOK), jnp.int32), pltpu.VMEM((8, 8, TOK), jnp.int32),
            pltpu.VMEM((C, 2 * E), F32),
            pltpu.VMEM((NZ, BLK, E), SUM_T), pltpu.VMEM((NZ, 8, E), F32),
            pltpu.VMEM((NZ, BLK, E), OUT_T), pltpu.VMEM((NZ, 8, E), F32),
            pltpu.VMEM((NZ - 1, BLK, E), SUM_T), pltpu.VMEM((NZ - 1, 8, E), F32),
            pltpu.VMEM((NZ - 1, BLK, E), OUT_T), pltpu.VMEM((NZ - 1, 8, E), F32),
            pltpu.VMEM((NZ, BLK, E), BF16), pltpu.VMEM((8, C // 2, TOK), F32),
            pltpu.VMEM((C // 2, E), F32), pltpu.VMEM((C // 2, E), F32), pltpu.VMEM((C // 2, E), F32),
            pltpu.VMEM((16, NZ, BLK, E), BF16), pltpu.VMEM((E, 2 * TOK), F32), pltpu.VMEM((2 * TOK, E), F32),
            pltpu.VMEM((NX, NY, E, 8 * E), BF16), pltpu.VMEM((2 * TOK, 16 * E), BF16),
            pltpu.VMEM((2 * TOK, 8 * E), F32), pltpu.VMEM((TOK, 8 * E), PAIR_T),
            pltpu.VMEM((TOK, 8 * E), PAIR_T),
            dma((144,)), dma((7,)), dma((7,)), dma((7,)), dma((7,)), dma((8,)),
            dma((7,)), dma((7,)), dma((7,)), dma((7,)), dma((7,)), dma((7,)),
            dma((16,)), dma((16,)), dma((4,)), dma((6,)),
            dma((16,)), dma(()), dma((4,)), dma((3,)), dma((2,)), dma((6,)), dma((6,)), dma((4,)), dma((3,)),
            pltpu.SemaphoreType.REGULAR, pltpu.SemaphoreType.REGULAR,
        ],
        compiler_params=pltpu.CompilerParams(
            collective_id=0, has_side_effects=True, vmem_limit_bytes=48 * 1024 * 1024
        ),
        cost_estimate=pl.CostEstimate(flops=4_000_000_000, bytes_accessed=200_000_000, transcendentals=1 << 20),
    )(queries, keys, values, ids, weight)


def on_device(queries, keys, values, cluster_ids, out_weight):
    q, k, v = (jnp.transpose(a, (1, 0, 2)) for a in (queries, keys, values))
    return chain(q, k, v, cluster_ids.T, out_weight)


def solution(mesh):
    placed = (
        P("seq", "head", None),
        P("seq", "head", None),
        P("seq", "head", None),
        P("seq", "head"),
        P("seq", "head"),
    )
    return jax.shard_map(
        on_device, mesh=mesh, in_specs=placed, out_specs=P("seq", "head"), check_vma=False
    )
```
